32 devices in a mesh: dp: 4 (over y, core), seq: 2 (over x), pool: 4 (over z).
Axes of the slice: x: 2, y: 2, z: 4, core: 2. Of those that a mesh axis runs over, the one named last changes fastest.
Arguments:
- events: bfloat16 [4096, 1024], P(('dp', 'seq', 'pool')), may hold values from -6 to 6
- input_weight: bfloat16 [1024, 4096], replicated, may hold values from -0.1875 to 0.1875
- output_weight: bfloat16 [1024, 1024], replicated, may hold values from -0.1875 to 0.1875
- positives: bfloat16 [4096, 1024], P(('dp', 'seq', 'pool')), may hold values from -8 to 8
- negatives: bfloat16 [512, 1024], P('pool'), may hold values from -6 to 6
- log_probs: bfloat16 [512], P('pool'), may hold values from -15 to -4
- lengths: int32 [32], replicated, may hold values from 1 to 256, 4096 in all
Outputs:
- d_events: float32 [4096, 1024], P(('dp', 'seq', 'pool'))
- d_output_weight: float32 [1024, 1024], P(('dp', 'seq'))
The draws below stay inside these ranges and needn't reach their ends.
Inputs may be any that keep to these rules, and one draw needn't show every extreme that they name: The histories lie end to end over all 4096 events, their lengths sum to 4096, and one history has exactly 256 events.
All inputs are finite; a program needn't handle non-finite values.
Results may differ from the reference program's by a relative error of at most 0.0095.
Values may be sent and summed in bfloat16 or wider, within the bound.
No kernel may reach another device: no remote copies, remote signals or barrier semaphores. Data moves between devices by JAX's collectives and lax.ppermute only.
A program may use at most 64 MiB of HBM per device.

```python
import math
import jax
import jax.numpy as jnp
import numpy as np
from jax import lax

D = 1024
HEADS = 8
EV_DEV = 128
REACH = 2
NEG_DEV = 128
LONGEST = 256
EVENTS = 4096
NEG = 512
USERS = 32


def event_rows_common(key):
    base_key = jax.random.fold_in(key, 7101)
    return jnp.clip(jax.random.normal(base_key, (EVENTS, D), jnp.float32), -6.0, 6.0)


def draw_events(key, part):
    return event_rows_common(key).astype(jnp.bfloat16)


def draw_positives(key, part):
    base_rows = event_rows_common(key)
    noise_rows = jnp.clip(jax.random.normal(jax.random.fold_in(key, 7202), (EVENTS, D), jnp.float32), -4.0, 4.0)
    top_share = 1.0
    mix_share = jax.random.uniform(jax.random.fold_in(key, 7203), (EVENTS, 1), jnp.float32, 0.0, top_share)
    return jnp.clip(base_rows + mix_share * noise_rows, -8.0, 8.0).astype(jnp.bfloat16)


def draw_log_probs(key, part):
    pool_count = NEG // NEG_DEV
    shard_span = max(pool_count - 1, 1)
    shard_index = (jnp.arange(NEG, dtype=jnp.int32) // NEG_DEV).astype(jnp.float32)
    rise_span = math.log(3.0)
    jitter = jax.random.uniform(jax.random.fold_in(key, 7301), (NEG,), jnp.float32, -1.0, 1.0)
    neg_log = 14.5 - math.log(NEG) + rise_span * shard_index / shard_span + jitter
    return (-neg_log).astype(jnp.bfloat16)


def steps_of(key, dims, cuts, low, high):
    gain = 1.0
    for dim, parts in cuts:
        steps = jax.random.uniform(jax.random.fold_in(jax.random.fold_in(key, 6), dim), (parts,), jnp.float32, low / len(cuts), high / len(cuts))
        gain = gain * jnp.repeat(jnp.exp(steps), dims[dim] // parts).reshape((-1,) + (1,) * (len(dims) - 1 - dim))
    return gain


def split_up(count, total, reach, skew):
    weights = [(1 << 20) // math.isqrt(grade ** skew) + 1 for grade in range(2, count + 1)]
    surplus, holding = total - reach - (count - 1), [1] * (count - 1)
    while surplus > 0:
        movable = [i for i in range(count - 1) if holding[i] < reach]
        mass, budget = sum([weights[i] for i in movable]), surplus
        for i in movable:
            more = min(reach - holding[i], max(1, budget * weights[i] // mass), surplus)
            holding[i] = holding[i] + more
            surplus = surplus - more
    return np.array([reach] + holding)


def ragged_sizes(stream_key, amount, total, bound, slope):
    if amount == 2:
        one = jax.random.randint(stream_key, (), max(1, total - bound), min(bound, total - 1) + 1)
        return jnp.stack([one, total - one])
    sizes = jnp.asarray(split_up(amount, total, bound, slope), jnp.int32)
    twos = (amount - 1) // 2
    giver, sink = sizes[1:1 + 2 * twos:2], sizes[2:2 + 2 * twos:2]
    room = jnp.minimum(giver - 1, bound - sink)
    passed = jax.random.randint(jax.random.fold_in(stream_key, 1), (twos,), 0, 1 << 20) % (room + 1)
    sizes = sizes.at[1:1 + 2 * twos:2].set(giver - passed).at[2:2 + 2 * twos:2].set(sink + passed)
    return sizes[jax.random.permutation(jax.random.fold_in(stream_key, 2), amount)]


def normal_values(own_key, dims, deviation, bound, split=(), kind=jnp.bfloat16):
    values = deviation * jax.random.normal(own_key, dims, jnp.float32)
    if split:
        values = values * steps_of(own_key, dims, split, -0.22, 0.18)
    return jnp.clip(values, -bound, bound).astype(kind)


def setup_inputs(seed: int = 0) -> dict:
    arg_keys = jax.random.split(jax.random.key(seed), 8)
    return {
        "events": draw_events(jax.random.fold_in(arg_keys[7], 71), 0),
        "input_weight": normal_values(arg_keys[1], (D, 4 * D), D ** -0.5, 0.1875),
        "output_weight": normal_values(arg_keys[2], (D, D), D ** -0.5, 0.1875),
        "positives": draw_positives(jax.random.fold_in(arg_keys[7], 71), 0),
        "negatives": normal_values(arg_keys[4], (NEG, D), 1.0, 6.0, ((0, 4),)),
        "log_probs": draw_log_probs(jax.random.fold_in(arg_keys[7], 71), 0),
        "lengths": ragged_sizes(arg_keys[6], USERS, EVENTS, LONGEST, 2).astype(jnp.int32),
    }


epsilon = 1e-05
sharpness_divisor = 0.05
loss_multiplier = 8.0

def normalize(row_data):
    centred = row_data - lax.optimization_barrier(jnp.mean(row_data, axis=1, keepdims=True))
    inv_std = lax.rsqrt(lax.optimization_barrier(jnp.mean(centred * centred, axis=1, keepdims=True)) + epsilon)
    return (centred * inv_std, inv_std)

def norm_back(grad_in, normed, inv_std):
    return (grad_in - lax.optimization_barrier(jnp.mean(grad_in, axis=1, keepdims=True)) - normed * lax.optimization_barrier(jnp.mean(grad_in * normed, axis=1, keepdims=True))) * inv_std

def silu_slope(values):
    sigmoid_v = jax.nn.sigmoid(values)
    return sigmoid_v * (1.0 + values * (1.0 - sigmoid_v))

def history_starts(lengths, first_row, row_count):
    starts = (jnp.cumsum(lengths) - lengths).astype(jnp.int32)
    positions = (first_row + jnp.arange(row_count, dtype=jnp.int32)).astype(jnp.int32)
    owner_start = lax.optimization_barrier(jnp.max(jnp.where(starts[None, :] <= positions[:, None], starts[None, :], 0), axis=1))
    return (owner_start, positions)

def visible(owner_start, positions, key_rows):
    allowed = (key_rows[None, :] >= owner_start[:, None]) & (key_rows[None, :] <= positions[:, None])
    return allowed.astype(jnp.float32)

def reference(events, input_weight, output_weight, positives, negatives, log_probs, lengths):
    feature_width = D
    row_count = EV_DEV
    reach_count = REACH
    block_count = EVENTS // EV_DEV
    head_size = feature_width // HEADS
    key_scale = 1.0 / math.sqrt(head_size)
    earlier_count = reach_count * row_count
    key_count = earlier_count + row_count
    event_blocks = events.reshape(block_count, row_count, feature_width)
    positive_blocks = positives.reshape(block_count, row_count, feature_width)
    negative_rows = negatives.astype(jnp.float32)
    sampled_decoy_vectors = (negative_rows * lax.rsqrt(lax.optimization_barrier(jnp.sum(negative_rows * negative_rows, axis=1, keepdims=True)))).astype(jnp.bfloat16)
    sequence_boundary_indices = log_probs.astype(jnp.float32)

    def project(block_idx):
        safe_idx = jnp.maximum(block_idx, 0).astype(jnp.int32)
        event_rows = lax.dynamic_index_in_dim(event_blocks, safe_idx, 0, keepdims=False).astype(jnp.float32)
        normed, inv_std = normalize(event_rows)
        return jnp.dot(normed.astype(jnp.bfloat16), input_weight, preferred_element_type=jnp.float32)

    def scan_step(state_in, block_idx):
        pre_stack, pending, weight_sum = state_in
        pre_act = pre_stack[0]
        event_rows = lax.dynamic_index_in_dim(event_blocks, block_idx, 0, keepdims=False).astype(jnp.float32)
        normed_x, inv_x = normalize(event_rows)
        oldest = project(block_idx - reach_count)
        prior_pres = jnp.concatenate([pre_stack[1:], oldest[None]], axis=0)
        prior_kv = jax.nn.silu(prior_pres[::-1]).astype(jnp.bfloat16)[:, :, 2 * feature_width:].reshape(earlier_count, 2 * feature_width)
        activated = jax.nn.silu(pre_act).astype(jnp.bfloat16)
        update_rows = activated[:, :feature_width]
        queries = activated[:, feature_width:2 * feature_width]
        key_values = activated[:, 2 * feature_width:]
        kv_all = jnp.concatenate([prior_kv, key_values], axis=0)
        keys_all = kv_all[:, :feature_width]
        values_all = kv_all[:, feature_width:]
        first_row = (block_idx * row_count).astype(jnp.int32)
        owner_start, positions = history_starts(lengths, first_row, row_count)
        key_rows = (first_row - earlier_count + jnp.arange(key_count, dtype=jnp.int32)).astype(jnp.int32)
        allowed = visible(owner_start, positions, key_rows)
        query_heads = queries.astype(jnp.float32).reshape(row_count, HEADS, head_size)
        key_heads = keys_all.astype(jnp.float32).reshape(key_count, HEADS, head_size)
        value_heads = values_all.astype(jnp.float32).reshape(key_count, HEADS, head_size)
        scores = jnp.einsum('ihd,jhd->hij', query_heads, key_heads) * key_scale
        weights = (jax.nn.silu(scores) * allowed[None] / EV_DEV).astype(jnp.bfloat16)
        mixed_out = jnp.einsum('hij,jhd->ihd', weights.astype(jnp.float32), value_heads).reshape(row_count, feature_width)
        normed_o, inv_o = normalize(mixed_out)
        update32 = update_rows.astype(jnp.float32)
        gated_rows = (normed_o * update32).astype(jnp.bfloat16)
        layer_out = jnp.dot(gated_rows, output_weight, preferred_element_type=jnp.float32) + event_rows
        inv_norm = lax.rsqrt(lax.optimization_barrier(jnp.sum(layer_out * layer_out, axis=1, keepdims=True)))
        normalized_result_vector = layer_out * inv_norm
        positive_rows = lax.dynamic_index_in_dim(positive_blocks, block_idx, 0, keepdims=False).astype(jnp.float32)
        target_normalized_vectors = positive_rows * lax.rsqrt(lax.optimization_barrier(jnp.sum(positive_rows * positive_rows, axis=1, keepdims=True)))
        target_similarity = lax.optimization_barrier(jnp.sum(normalized_result_vector * target_normalized_vectors, axis=1)) / sharpness_divisor
        similarity_values_matrix = jnp.dot(normalized_result_vector.astype(jnp.bfloat16), sampled_decoy_vectors.T, preferred_element_type=jnp.float32) / sharpness_divisor - sequence_boundary_indices[None, :]
        exp_terms = jnp.exp(similarity_values_matrix)
        target_exp_term = jnp.exp(target_similarity)
        partition_denominator = target_exp_term + lax.optimization_barrier(jnp.sum(exp_terms, axis=1))
        probability_mixed_vectors = jnp.dot(exp_terms.astype(jnp.bfloat16), sampled_decoy_vectors, preferred_element_type=jnp.float32)
        derivative_normalized_matrix = loss_multiplier / sharpness_divisor * (probability_mixed_vectors / partition_denominator[:, None] + (target_exp_term / partition_denominator - 1.0)[:, None] * target_normalized_vectors)
        grad_out = (derivative_normalized_matrix - normalized_result_vector * lax.optimization_barrier(jnp.sum(normalized_result_vector * derivative_normalized_matrix, axis=1, keepdims=True))) * inv_norm
        grad_low = grad_out.astype(jnp.bfloat16)
        weight_term = jnp.dot(gated_rows.T, grad_low, preferred_element_type=jnp.float32)
        grad_gated = jnp.dot(grad_low, output_weight.T, preferred_element_type=jnp.float32)
        grad_update = grad_gated * normed_o
        grad_normed = grad_gated * update32
        grad_mixed = norm_back(grad_normed, normed_o, inv_o).astype(jnp.bfloat16)
        grad_heads = grad_mixed.astype(jnp.float32).reshape(row_count, HEADS, head_size)
        grad_values = jnp.einsum('hij,ihd->jhd', weights.astype(jnp.float32), grad_heads).reshape(key_count, feature_width)
        grad_weights = jnp.einsum('ihd,jhd->hij', grad_heads, value_heads)
        grad_scores = (grad_weights * allowed[None] / EV_DEV * silu_slope(scores)).astype(jnp.bfloat16)
        grad_scores32 = grad_scores.astype(jnp.float32)
        grad_query = jnp.einsum('hij,jhd->ihd', grad_scores32, key_heads).reshape(row_count, feature_width) * key_scale
        grad_keys = jnp.einsum('hij,ihd->jhd', grad_scores32, query_heads).reshape(key_count, feature_width) * key_scale
        grad_kv = jnp.concatenate([grad_keys, grad_values], axis=1).reshape(reach_count + 1, row_count, 2 * feature_width)
        own_kv = grad_kv[reach_count] + pending[0]
        carried = jnp.concatenate([pending[1:], jnp.zeros((1, row_count, 2 * feature_width), jnp.float32)], axis=0)
        new_pending = carried + grad_kv[:reach_count][::-1]
        grad_act = jnp.concatenate([grad_update, grad_query, own_kv], axis=1)
        grad_pre = (grad_act * silu_slope(pre_act)).astype(jnp.bfloat16)
        grad_x = jnp.dot(grad_pre, input_weight.T, preferred_element_type=jnp.float32)
        grad_block = norm_back(grad_x, normed_x, inv_x) + grad_out
        return ((prior_pres, new_pending, weight_sum + weight_term), grad_block)
    start_stack = jnp.stack([project(jnp.int32(block_count - 1 - back_index)) for back_index in range(reach_count)], axis=0)
    initial = (start_stack, jnp.zeros((reach_count, row_count, 2 * feature_width), jnp.float32), jnp.zeros((feature_width, feature_width), jnp.float32))
    final_state, grad_blocks = lax.scan(scan_step, initial, jnp.arange(block_count, dtype=jnp.int32), reverse=True)
    return (grad_blocks.reshape(EVENTS, feature_width), final_state[2])
```

```python
import functools
import math

import jax
import jax.numpy as jnp
from jax import lax
from jax.experimental import pallas as pl
from jax.experimental.pallas import tpu as pltpu
from jax.sharding import PartitionSpec as P

HEADS = 8
EV_DEV = 128
REACH = 2

epsilon = 1e-05
sharpness_divisor = 0.05
loss_multiplier = 8.0

ALL = ("dp", "seq", "pool")
PLANE = ("dp", "seq")
BF = jnp.bfloat16
F32 = jnp.float32

NT = (((1,), (1,)), ((), ()))
TN = (((0,), (0,)), ((), ()))


def dot(a, b):
    return jnp.dot(a, b, preferred_element_type=F32)


def dot_nt(a, b):
    return lax.dot_general(a, b, NT, preferred_element_type=F32)


def dot_tn(a, b):
    return lax.dot_general(a, b, TN, preferred_element_type=F32)


def shifted(x, by):
    length = lax.axis_size(ALL)
    pairs = [(i, i + by) for i in range(length) if 0 <= i + by < length]
    return lax.ppermute(x, ALL, pairs)


def is_pow2(n):
    return n & (n - 1) == 0


def swapped(x, axis, bit):
    return lax.ppermute(x, axis, [(i, i ^ bit) for i in range(lax.axis_size(axis))])


def gathered(x, axis):
    n = lax.axis_size(axis)
    if not is_pow2(n):
        return jnp.concatenate(
            [x] + [lax.ppermute(x, axis, [(i, (i + k) % n) for i in range(n)]) for k in range(1, n)],
            axis=0,
        )
    bits = [1 << b for b in range(n.bit_length() - 1)]
    if axis == "dp":
        bits = bits[::-1]
    for bit in bits:
        x = jnp.concatenate([x, swapped(x, axis, bit)], axis=0)
    return x


def normalize(row_data):
    centred = row_data - jnp.mean(row_data, axis=1, keepdims=True)
    inv_std = lax.rsqrt(jnp.mean(centred * centred, axis=1, keepdims=True) + epsilon)
    return centred * inv_std, inv_std


def norm_back(grad_in, normed, inv_std):
    return (
        grad_in
        - jnp.mean(grad_in, axis=1, keepdims=True)
        - normed * jnp.mean(grad_in * normed, axis=1, keepdims=True)
    ) * inv_std


def silu_and_slope(v):
    sig = jax.nn.sigmoid(v)
    return v * sig, sig * (1.0 + v * (1.0 - sig))


def own_kernel(x_ref, w_ref, act_ref, slope_ref, xn_ref):
    @pl.when(pl.program_id(0) == 0)
    def _():
        xn_ref[...] = normalize(x_ref[...].astype(F32))[0].astype(BF)

    act, slope = silu_and_slope(dot(xn_ref[...], w_ref[...]))
    act_ref[...] = act.astype(BF)
    slope_ref[...] = slope.astype(BF)


def forward_kernel(
    place_ref, e1_ref, e2_ref, ev_ref, pos_ref, neg_ref, owner_ref, q_ref, k_ref, v_ref,
    su_ref, up_ref, wk_ref, wv_ref, wo_ref,
    kh_ref, vh_ref, w_ref, sl_ref, mine_ref, pay_ref, gout_ref, gpu_ref, gm_ref,
    xn_ref, mixed_ref, gated_ref, *, heads_step, scale, plane_cols,
):
    step = pl.program_id(0)
    rows, width = ev_ref.shape
    early = xn_ref.shape[0]
    keys = early + rows
    hd = k_ref.shape[1] // heads_step

    @pl.when(step == 0)
    def _():
        xn_ref[0:rows, :] = normalize(e2_ref[...].astype(F32))[0].astype(BF)
        xn_ref[rows:, :] = normalize(e1_ref[...].astype(F32))[0].astype(BF)

    xn = xn_ref[...]
    kh = jax.nn.silu(dot(xn, wk_ref[...])).astype(BF)
    vh = jax.nn.silu(dot(xn, wv_ref[...])).astype(BF)
    kh_ref[...] = kh
    vh_ref[...] = vh
    col = lax.broadcasted_iota(jnp.int32, (rows, keys), 1)
    row = lax.broadcasted_iota(jnp.int32, (rows, keys), 0)
    allowed = (col >= owner_ref[...] + early) & (col <= row + early)
    share = jnp.where(allowed, 1.0 / EV_DEV, 0.0)
    for h in range(heads_step):
        c = slice(h * hd, (h + 1) * hd)
        key = jnp.concatenate([kh[:, c], k_ref[:, c]], axis=0)
        val = jnp.concatenate([vh[:, c], v_ref[:, c]], axis=0)
        act, slope = silu_and_slope(dot_nt(q_ref[:, c], key) * scale)
        wts = (act * share).astype(BF)
        w_ref[h] = wts
        sl_ref[h] = (slope * share).astype(BF)
        at = pl.multiple_of((step * heads_step + h) * hd, hd)
        mixed_ref[:, pl.ds(at, hd)] = dot(wts, val)

    @pl.when(step == pl.num_programs(0) - 1)
    def _():
        event_rows = ev_ref[...].astype(F32)
        normed_o, inv_o = normalize(mixed_ref[...])
        update = up_ref[...].astype(F32)
        gated = (normed_o * update).astype(BF)
        gated_ref[...] = gated
        core, group = place_ref[0], place_ref[1]
        seq_n = place_ref[2]
        half = plane_cols // 2
        per = width // plane_cols if half else 0
        if not half:
            mine_ref[...] = gated
        for j in range(half):
            g = group ^ j
            base = (g // seq_n) * 2 * seq_n + lax.rem(g, seq_n)
            a0 = pl.multiple_of((base + core * seq_n) * per, per)
            a1 = pl.multiple_of((base + (1 - core) * seq_n) * per, per)
            mine_ref[:, j * per:(j + 1) * per] = gated_ref[:, pl.ds(a0, per)]
            pay_ref[:, j * per:(j + 1) * per] = gated_ref[:, pl.ds(a1, per)]
        layer_out = dot(gated, wo_ref[...]) + event_rows
        inv_norm = lax.rsqrt(jnp.sum(layer_out * layer_out, axis=1, keepdims=True))
        unit = layer_out * inv_norm
        positive = pos_ref[...].astype(F32)
        target = positive * lax.rsqrt(jnp.sum(positive * positive, axis=1, keepdims=True))
        pos_logit = jnp.sum(unit * target, axis=1, keepdims=True) / sharpness_divisor
        neg = neg_ref[:, :width]
        lane = lax.broadcasted_iota(jnp.int32, (rows, neg_ref.shape[1] - width), 1)
        first = jnp.where(lane == 0, 1.0, 0.0).astype(BF)
        offset = dot_nt(first, neg_ref[:, width:])
        neg_logit = dot_nt(unit.astype(BF), neg) / sharpness_divisor - offset
        exp_terms = jnp.exp(neg_logit)
        pos_exp = jnp.exp(pos_logit)
        total = pos_exp + jnp.sum(exp_terms, axis=1, keepdims=True)
        weighted = dot(exp_terms.astype(BF), neg)
        grad_unit = (loss_multiplier / sharpness_divisor) * (
            weighted / total + (pos_exp / total - 1.0) * target
        )
        grad_out = (
            grad_unit - unit * jnp.sum(unit * grad_unit, axis=1, keepdims=True)
        ) * inv_norm
        gout_ref[...] = grad_out
        low = grad_out.astype(BF)
        pay_ref[:, half * per:] = low
        grad_gated = dot_nt(low, wo_ref[...])
        gpu_ref[...] = (grad_gated * normed_o * su_ref[...].astype(F32)).astype(BF)
        gm_ref[...] = norm_back(grad_gated * update, normed_o, inv_o).astype(BF)


def product_kernel(mine_ref, pay_ref, got_ref, own_ref, send_ref):
    rows = mine_ref.shape[0]
    blocks = send_ref.shape[0] + 1
    per = mine_ref.shape[1] // blocks
    cols = mine_ref.shape[1]
    low = jnp.concatenate([pay_ref[:, cols:], got_ref[:, cols:]], axis=0)
    gated = jnp.concatenate([mine_ref[...], got_ref[:, :cols]], axis=0)
    out = dot_tn(gated, low)
    own_ref[...] = out[:per]
    for j in range(1, blocks):
        send_ref[j - 1] = out[j * per:(j + 1) * per].astype(BF)


def middle_kernel(
    l1_ref, l2_ref, owner_ref, q_ref, k_ref, v_ref, kh_ref, vh_ref, w_ref, sl_ref, gm_ref,
    sq_ref, gpu_ref, wu_ref, wq_ref,
    qn_ref, wn_ref, sn_ref, dk_ref, dv_ref, gx_ref,
    xn_ref, *, heads_step, scale,
):
    step = pl.program_id(0)
    rows = q_ref.shape[0]
    early = kh_ref.shape[0]
    later = xn_ref.shape[0]
    hd = k_ref.shape[1] // heads_step

    @pl.when(step == 0)
    def _():
        xn_ref[0:rows, :] = normalize(l1_ref[...].astype(F32))[0].astype(BF)
        xn_ref[rows:, :] = normalize(l2_ref[...].astype(F32))[0].astype(BF)
        gx_ref[...] = jnp.zeros_like(gx_ref)

    qn = jax.nn.silu(dot(xn_ref[...], wq_ref[...])).astype(BF)
    qn_ref[...] = qn
    col = lax.broadcasted_iota(jnp.int32, (later, rows), 1)
    share = jnp.where(col >= owner_ref[...], 1.0 / EV_DEV, 0.0)
    grad_q = []
    for h in range(heads_step):
        c = slice(h * hd, (h + 1) * hd)
        act, slope = silu_and_slope(dot_nt(qn[:, c], k_ref[:, c]) * scale)
        wn_ref[:, c] = (act * share).astype(BF)
        sn_ref[:, c] = (slope * share).astype(BF)
        gm = gm_ref[:, c]
        key = jnp.concatenate([kh_ref[:, c], k_ref[:, c]], axis=0)
        val = jnp.concatenate([vh_ref[:, c], v_ref[:, c]], axis=0)
        ds = (dot_nt(gm, val) * sl_ref[h].astype(F32)).astype(BF)
        grad_q.append(dot(ds, key) * scale)
        dk_ref[:, c] = dot_tn(ds[:, early:], q_ref[:, c])
        dv_ref[:, c] = dot_tn(w_ref[h][:, early:], gm)
    gpq = (jnp.concatenate(grad_q, axis=1) * sq_ref[...].astype(F32)).astype(BF)
    gx_ref[...] += dot_nt(gpu_ref[...], wu_ref[...]) + dot_nt(gpq, wq_ref[...])


def last_kernel(
    ev_ref, g1_ref, g2_ref, qn_ref, wn_ref, sn_ref, k_ref, v_ref, dk_ref, dv_ref,
    sk_ref, sv_ref, wk_ref, wv_ref, gx_ref, gout_ref, out_ref, *, heads_step, scale,
):
    step = pl.program_id(0)
    hd = k_ref.shape[1] // heads_step

    @pl.when(step == 0)
    def _():
        out_ref[...] = gx_ref[...]

    grad_k, grad_v = [], []
    for h in range(heads_step):
        c = slice(h * hd, (h + 1) * hd)
        gm = jnp.concatenate([g1_ref[:, c], g2_ref[:, c]], axis=0)
        ds = (dot_nt(gm, v_ref[:, c]) * sn_ref[:, c].astype(F32)).astype(BF)
        grad_k.append(dot_tn(ds, qn_ref[:, c]))
        grad_v.append(dot_tn(wn_ref[:, c], gm))
    gk = (dk_ref[...] + jnp.concatenate(grad_k, axis=1)) * scale
    gv = dv_ref[...] + jnp.concatenate(grad_v, axis=1)
    gpk = (gk * sk_ref[...].astype(F32)).astype(BF)
    gpv = (gv * sv_ref[...].astype(F32)).astype(BF)
    out_ref[...] += dot_nt(gpk, wk_ref[...]) + dot_nt(gpv, wv_ref[...])

    @pl.when(step == pl.num_programs(0) - 1)
    def _():
        normed_x, inv_x = normalize(ev_ref[...].astype(F32))
        out_ref[...] = norm_back(out_ref[...], normed_x, inv_x) + gout_ref[...]


def full(shape):
    return pl.BlockSpec(shape, lambda *_: (0,) * len(shape))


def cols(rows, width, base):
    return pl.BlockSpec((rows, width), lambda i, *_: (0, base + i))


def shaped(shape, dtype):
    return jax.ShapeDtypeStruct(shape, dtype)


def shards(events, input_weight, output_weight, positives, negatives, log_probs, lengths):
    rows, width = events.shape
    hd = width // HEADS
    scale = 1.0 / math.sqrt(hd)
    early = REACH * rows
    keys = early + rows
    heads_step = 2
    steps = HEADS // heads_step
    tile = heads_step * hd
    per_part = width // tile

    dp_n, seq_n = lax.axis_size("dp"), lax.axis_size("seq")
    plane_n = dp_n * seq_n
    half = plane_n // 2
    dp_i, seq_i = lax.axis_index("dp"), lax.axis_index("seq")
    core = lax.rem(dp_i, 2)
    group = (dp_i // 2) * seq_n + seq_i
    place = jnp.stack([core, group, jnp.int32(seq_n)]).astype(jnp.int32)
    paired = width % (plane_n * 128) == 0 and is_pow2(half) and half > 0
    sent = width // 2 if paired else 0

    e1 = shifted(events, 1)
    e2 = shifted(events, 2)
    l1 = shifted(events, -1)
    l2 = shifted(events, -2)

    negative_rows = negatives.astype(F32)
    neg_unit = (
        negative_rows * lax.rsqrt(jnp.sum(negative_rows * negative_rows, axis=1, keepdims=True))
    ).astype(BF)
    neg_ext = jnp.concatenate(
        [neg_unit, jnp.broadcast_to(log_probs[:, None], (negatives.shape[0], 128))], axis=1
    )
    part = negatives.shape[0] // plane_n
    piece = lax.dynamic_slice_in_dim(neg_ext, (dp_i * seq_n + seq_i) * part, part, 0)
    neg_all = gathered(gathered(gathered(piece, "pool"), "seq"), "dp")

    first_row = lax.axis_index(ALL) * rows
    starts = jnp.cumsum(lengths) - lengths
    positions = first_row + jnp.arange(keys, dtype=jnp.int32)
    owner = jnp.max(
        jnp.where(starts[None, :] <= positions[:, None], starts[None, :], 0), axis=1, keepdims=True
    )
    owner = (owner - first_row).astype(jnp.int32)

    own_tile = width // 2
    act, slope = pl.pallas_call(
        own_kernel,
        grid=(4 * width // own_tile,),
        in_specs=[full((rows, width)), cols(width, own_tile, 0)],
        out_specs=[cols(rows, own_tile, 0), cols(rows, own_tile, 0)],
        out_shape=[shaped((rows, 4 * width), BF), shaped((rows, 4 * width), BF)],
        scratch_shapes=[pltpu.VMEM((rows, width), BF)],
        name="own",
    )(events, input_weight)

    head_spec = pl.BlockSpec((heads_step, rows, keys), lambda i, *_: (i, 0, 0))
    neg_shape = neg_all.shape
    kh, vh, wts, slopes, mine, pay, grad_out, gpu, gm = pl.pallas_call(
        functools.partial(
            forward_kernel, heads_step=heads_step, scale=scale, plane_cols=plane_n if paired else 0
        ),
        grid_spec=pltpu.PrefetchScalarGridSpec(
            num_scalar_prefetch=1,
            grid=(steps,),
            in_specs=[
                full((rows, width)), full((rows, width)), full((rows, width)),
                full((rows, width)), full(neg_shape), full((rows, 1)),
                cols(rows, tile, per_part), cols(rows, tile, 2 * per_part),
                cols(rows, tile, 3 * per_part),
                full((rows, width)), full((rows, width)),
                cols(width, tile, 2 * per_part), cols(width, tile, 3 * per_part),
                full((width, width)),
            ],
            out_specs=[
                cols(early, tile, 0), cols(early, tile, 0), head_spec, head_spec,
                full((rows, sent or width)), full((rows, sent + width)),
                full((rows, width)), full((rows, width)), full((rows, width)),
            ],
            scratch_shapes=[
                pltpu.VMEM((early, width), BF), pltpu.VMEM((rows, width), F32),
                pltpu.VMEM((rows, width), BF),
            ],
        ),
        out_shape=[
            shaped((early, width), BF), shaped((early, width), BF),
            shaped((HEADS, rows, keys), BF), shaped((HEADS, rows, keys), BF),
            shaped((rows, sent or width), BF), shaped((rows, sent + width), BF),
            shaped((rows, width), F32), shaped((rows, width), BF), shaped((rows, width), BF),
        ],
        name="forward",
    )(
        place, e1, e2, events, positives, neg_all, owner[:rows], act, act, act, slope, act,
        input_weight, input_weight, output_weight,
    )

    g1 = shifted(gm, -1)
    g2 = shifted(gm, -2)
    if paired:
        got = swapped(pay, "dp", 1)
        own_sum, sends = pl.pallas_call(
            product_kernel,
            out_shape=[
                shaped((width // plane_n, width), F32),
                shaped((half - 1, width // plane_n, width), BF),
            ],
            name="product",
        )(mine, pay, got)

    qn, wn, sn, dk, dv, gx = pl.pallas_call(
        functools.partial(middle_kernel, heads_step=heads_step, scale=scale),
        grid=(steps,),
        in_specs=[
            full((rows, width)), full((rows, width)), full((early, 1)),
            cols(rows, tile, per_part), cols(rows, tile, 2 * per_part),
            cols(rows, tile, 3 * per_part),
            cols(early, tile, 0), cols(early, tile, 0), head_spec, head_spec,
            cols(rows, tile, 0), cols(rows, tile, per_part), cols(rows, tile, 0),
            cols(width, tile, 0), cols(width, tile, per_part),
        ],
        out_specs=[
            cols(early, tile, 0), cols(early, tile, 0), cols(early, tile, 0),
            cols(rows, tile, 0), cols(rows, tile, 0), full((rows, width)),
        ],
        out_shape=[
            shaped((early, width), BF), shaped((early, width), BF), shaped((early, width), BF),
            shaped((rows, width), F32), shaped((rows, width), F32), shaped((rows, width), F32),
        ],
        scratch_shapes=[pltpu.VMEM((early, width), BF)],
        name="middle",
    )(
        l1, l2, owner[rows:], act, act, act, kh, vh, wts, slopes, gm, slope, gpu,
        input_weight, input_weight,
    )

    if paired:
        total = own_sum
        for j in range(1, half):
            pairs = []
            for i in range(plane_n):
                d, q = divmod(i, seq_n)
                t = ((d // 2) * seq_n + q) ^ j
                pairs.append((i, ((t // seq_n) * 2 + d % 2) * seq_n + t % seq_n))
            total = total + lax.ppermute(sends[j - 1], PLANE, pairs).astype(F32)
    else:
        total = lax.psum_scatter(dot_tn(mine, pay), PLANE, scatter_dimension=0, tiled=True)
    pool_n = lax.axis_size("pool")
    if is_pow2(pool_n):
        for b in range(pool_n.bit_length() - 1):
            low = total.astype(BF)
            total = low.astype(F32) + swapped(low, "pool", 1 << b).astype(F32)
    else:
        total = lax.psum(total, "pool")

    d_events = pl.pallas_call(
        functools.partial(last_kernel, heads_step=heads_step, scale=scale),
        grid=(steps,),
        in_specs=[
            full((rows, width)), cols(rows, tile, 0), cols(rows, tile, 0),
            cols(early, tile, 0), cols(early, tile, 0), cols(early, tile, 0),
            cols(rows, tile, 2 * per_part), cols(rows, tile, 3 * per_part),
            cols(rows, tile, 0), cols(rows, tile, 0),
            cols(rows, tile, 2 * per_part), cols(rows, tile, 3 * per_part),
            cols(width, tile, 2 * per_part), cols(width, tile, 3 * per_part),
            full((rows, width)), full((rows, width)),
        ],
        out_specs=full((rows, width)),
        out_shape=shaped((rows, width), F32),
        name="last",
    )(
        events, g1, g2, qn, wn, sn, act, act, dk, dv, slope, slope,
        input_weight, input_weight, gx, grad_out,
    )
    return (d_events, total)


def solution(mesh):
    placed = (
        P(("dp", "seq", "pool"), None),
        P(),
        P(),
        P(("dp", "seq", "pool"), None),
        P("pool", None),
        P("pool"),
        P(),
    )
    return jax.shard_map(
        shards,
        mesh=mesh,
        in_specs=placed,
        out_specs=(P(("dp", "seq", "pool"), None), P(("dp", "seq"), None)),
        check_vma=False,
    )
```

```python
import functools
import math

import jax
import jax.numpy as jnp
from jax import lax
from jax.experimental import pallas as pl
from jax.experimental.pallas import tpu as pltpu
from jax.sharding import PartitionSpec as P


HEADS = 8
EV_DEV = 128
REACH = 2

epsilon = 1e-05
sharpness_divisor = 0.05
loss_multiplier = 8.0

ALL = ("dp", "seq", "pool")
PLANE = ("dp", "seq")
VMEM_BYTES = 16 << 20
BF = jnp.bfloat16
F32 = jnp.float32

NT = (((1,), (1,)), ((), ()))
TN = (((0,), (0,)), ((), ()))


def dot(a, b):
    return jnp.dot(a, b, preferred_element_type=F32)


def dot_nt(a, b):
    return lax.dot_general(a, b, NT, preferred_element_type=F32)


def dot_tn(a, b):
    return lax.dot_general(a, b, TN, preferred_element_type=F32)


def shifted(x, by):
    length = lax.axis_size(ALL)
    pairs = [(i, i + by) for i in range(length) if 0 <= i + by < length]
    return lax.ppermute(x, ALL, pairs)


def neighbours(x):
    n = lax.axis_size(ALL)
    two = lax.ppermute(x, ALL, [(i, i ^ 2) for i in range(n)])
    odd = [(i, i + 1) for i in range(1, n - 1, 2)]
    cross = lax.ppermute(x, ALL, odd + [(j, i) for i, j in odd])
    one = lax.ppermute(x, ALL, [(i, i ^ 1) for i in range(n)])
    if lax.axis_size("pool") == 4:
        source, by = two, 4
    else:
        source, by = x, -2
    pairs = [(i, i + by if i % 4 < 2 else i - by) for i in range(n)]
    far = lax.ppermute(source, ALL, [(i, j) for i, j in pairs if 0 <= j < n])
    return one, cross, two, far


def is_pow2(n):
    return n & (n - 1) == 0


def swapped(x, axis, bit):
    return lax.ppermute(x, axis, [(i, i ^ bit) for i in range(lax.axis_size(axis))])


def gather_stages(sizes):
    stages = []
    for axis in ("pool", "seq", "dp"):
        bits = [1 << b for b in range(sizes[axis].bit_length() - 1)]
        stages += [(axis, bit) for bit in (bits[::-1] if axis == "dp" else bits)]
    return stages


def gathered(x):
    sizes = {axis: lax.axis_size(axis) for axis in ALL}
    if all(is_pow2(n) for n in sizes.values()):
        parts = [x]
        for axis, bit in gather_stages(sizes):
            x = jnp.concatenate(parts, axis=0) if len(parts) > 1 else x
            parts = [x, swapped(x, axis, bit)]
        return parts
    for axis, n in sizes.items():
        turns = [lax.ppermute(x, axis, [(i, (i + k) % n) for i in range(n)]) for k in range(1, n)]
        x = jnp.concatenate([x] + turns, axis=0)
    return [x[:x.shape[0] // 2], x[x.shape[0] // 2:]]


def normalize(row_data):
    centred = row_data - jnp.mean(row_data, axis=1, keepdims=True)
    inv_std = lax.rsqrt(jnp.mean(centred * centred, axis=1, keepdims=True) + epsilon)
    return centred * inv_std, inv_std


def norm_back(grad_in, normed, inv_std):
    return (
        grad_in
        - jnp.mean(grad_in, axis=1, keepdims=True)
        - normed * jnp.mean(grad_in * normed, axis=1, keepdims=True)
    ) * inv_std


def silu_and_slope(v):
    sig = jax.nn.sigmoid(v)
    return v * sig, sig * (1.0 + v * (1.0 - sig))


def own_kernel(x_ref, w_ref, *out_refs):
    width = x_ref.shape[1]
    parts = len(out_refs) // 2
    xn = normalize(x_ref[...].astype(F32))[0].astype(BF)
    for i in range(parts):
        act, slope = silu_and_slope(dot(xn, w_ref[:, i * width:(i + 1) * width]))
        out_refs[i][...] = act.astype(BF)
        out_refs[parts + i][...] = slope.astype(BF)


def history_ends(lengths_ref, first, shape):
    column = first + lax.broadcasted_iota(jnp.int32, shape, 1)
    far = jnp.full(shape, jnp.iinfo(jnp.int32).max, jnp.int32)

    def body(u, carry):
        end, found = carry
        end = end + lengths_ref[u]
        return end, jnp.minimum(found, jnp.where(end > column, end, far))

    found = lax.fori_loop(0, lengths_ref.shape[0], body, (jnp.int32(0), far))[1]
    return jnp.where(column >= 0, found, 0)


def piece_kernel(neg_ref, log_ref, out_ref):
    part = out_ref.shape[0]
    width = neg_ref.shape[1]
    at = pl.multiple_of(lax.axis_index(PLANE) * part, part)
    raw = neg_ref[pl.ds(at, part), :].astype(F32)
    out_ref[:, :width] = (
        raw * lax.rsqrt(jnp.sum(raw * raw, axis=1, keepdims=True))
    ).astype(BF)
    logs = log_ref[...].astype(F32)
    shape = (part, logs.shape[1])
    wanted = lax.broadcasted_iota(jnp.int32, shape, 1) == at + lax.broadcasted_iota(
        jnp.int32, shape, 0
    )
    mine = jnp.sum(jnp.where(wanted, logs, 0.0), axis=1, keepdims=True)
    out_ref[:, width:] = jnp.broadcast_to(mine, (part, 128)).astype(BF)


def attend_kernel(
    lengths_ref, one_ref, cross_ref, two_ref, far_ref, q_ref, k_ref, v_ref, w_ref,
    kh_ref, vh_ref, wt_ref, sl_ref, mixed_ref, *, heads, scale,
):
    rows, width = q_ref.shape
    early = kh_ref.shape[0]
    keys = early + rows
    hd = width // heads
    device = lax.axis_index(ALL)
    first_row = device * rows
    e2 = jnp.where(lax.rem(device, 4) < 2, far_ref[...].astype(F32), two_ref[...].astype(F32))
    e1 = jnp.where(lax.rem(device, 2) == 1, one_ref[...].astype(F32), cross_ref[...].astype(F32))
    xn = jnp.concatenate([normalize(e)[0].astype(BF) for e in (e2, e1)], axis=0)
    kh_ref[...] = jax.nn.silu(dot(xn, w_ref[:, 2 * width:3 * width])).astype(BF)
    vh_ref[...] = jax.nn.silu(dot(xn, w_ref[:, 3 * width:])).astype(BF)
    ends = history_ends(lengths_ref, first_row - early, (8, keys))[0:1]
    col = lax.broadcasted_iota(jnp.int32, (rows, keys), 1)
    row = lax.broadcasted_iota(jnp.int32, (rows, keys), 0)
    allowed = (row + first_row < ends) & (col <= row + early)
    share = jnp.where(allowed, 1.0 / EV_DEV, 0.0)
    for h in range(heads):
        c = slice(h * hd, (h + 1) * hd)
        key = jnp.concatenate([kh_ref[:, c], k_ref[:, c]], axis=0)
        val = jnp.concatenate([vh_ref[:, c], v_ref[:, c]], axis=0)
        act, slope = silu_and_slope(dot_nt(q_ref[:, c], key) * scale)
        wts = (act * share).astype(BF)
        wt_ref[h] = wts
        sl_ref[h] = (slope * share).astype(BF)
        mixed_ref[:, c] = dot(wts, val)


def loss_kernel(
    mixed_ref, ev_ref, pos_ref, neg0_ref, neg1_ref, su_ref, up_ref, wo_ref,
    mine_ref, pay_ref, gout_ref, gpu_ref, gm_ref, gated_ref, *, plane_cols,
):
    rows, width = ev_ref.shape
    event_rows = ev_ref[...].astype(F32)
    normed_o, inv_o = normalize(mixed_ref[...])
    update = up_ref[...].astype(F32)
    gated = (normed_o * update).astype(BF)
    gated_ref[...] = gated
    dp_i, seq_n = lax.axis_index("dp"), lax.axis_size("seq")
    core = lax.rem(dp_i, 2)
    group = (dp_i // 2) * seq_n + lax.axis_index("seq")
    half = plane_cols // 2
    per = width // plane_cols if half else 0
    if not half:
        mine_ref[...] = gated
    for j in range(half):
        g = group ^ j
        base = (g // seq_n) * 2 * seq_n + lax.rem(g, seq_n)
        a0 = pl.multiple_of((base + core * seq_n) * per, per)
        a1 = pl.multiple_of((base + (1 - core) * seq_n) * per, per)
        mine_ref[:, j * per:(j + 1) * per] = gated_ref[:, pl.ds(a0, per)]
        pay_ref[:, j * per:(j + 1) * per] = gated_ref[:, pl.ds(a1, per)]
    layer_out = dot(gated, wo_ref[...]) + event_rows
    inv_norm = lax.rsqrt(jnp.sum(layer_out * layer_out, axis=1, keepdims=True))
    unit = layer_out * inv_norm
    positive = pos_ref[...].astype(F32)
    target = positive * lax.rsqrt(jnp.sum(positive * positive, axis=1, keepdims=True))
    pos_logit = jnp.sum(unit * target, axis=1, keepdims=True) / sharpness_divisor
    neg = jnp.concatenate([neg0_ref[:, :width], neg1_ref[:, :width]], axis=0)
    logs = jnp.concatenate([neg0_ref[:, width:], neg1_ref[:, width:]], axis=0)
    lane = lax.broadcasted_iota(jnp.int32, (rows, logs.shape[1]), 1)
    offset = dot_nt(jnp.where(lane == 0, 1.0, 0.0).astype(BF), logs)
    neg_logit = dot_nt(unit.astype(BF), neg) / sharpness_divisor - offset
    exp_terms = jnp.exp(neg_logit)
    pos_exp = jnp.exp(pos_logit)
    total = pos_exp + jnp.sum(exp_terms, axis=1, keepdims=True)
    weighted = dot(exp_terms.astype(BF), neg)
    grad_unit = (loss_multiplier / sharpness_divisor) * (
        weighted / total + (pos_exp / total - 1.0) * target
    )
    grad_out = (grad_unit - unit * jnp.sum(unit * grad_unit, axis=1, keepdims=True)) * inv_norm
    gout_ref[...] = grad_out
    low = grad_out.astype(BF)
    pay_ref[:, half * per:] = low
    grad_gated = dot_nt(low, wo_ref[...])
    gpu_ref[...] = (grad_gated * normed_o * su_ref[...].astype(F32)).astype(BF)
    gm_ref[...] = norm_back(grad_gated * update, normed_o, inv_o).astype(BF)


def product_kernel(mine_ref, pay_ref, got_ref, own_ref, *send_refs):
    cols = mine_ref.shape[1]
    per = cols // (len(send_refs) + 1)
    low = jnp.concatenate([pay_ref[:, cols:], got_ref[:, cols:]], axis=0)
    gated = jnp.concatenate([mine_ref[...], got_ref[:, :cols]], axis=0)
    out = dot_tn(gated, low)
    own_ref[...] = out[:per]
    for j, send_ref in enumerate(send_refs, 1):
        send_ref[...] = out[j * per:(j + 1) * per].astype(BF)


def later_kernel(
    lengths_ref, one_ref, cross_ref, two_ref, far_ref, k_ref, w_ref,
    qn_ref, wn_ref, sn_ref, *, heads, scale,
):
    rows, width = k_ref.shape
    later = wn_ref.shape[0]
    hd = width // heads
    device = lax.axis_index(ALL)
    first_row = device * rows
    l1 = jnp.where(lax.rem(device, 2) == 1, cross_ref[...].astype(F32), one_ref[...].astype(F32))
    l2 = jnp.where(lax.rem(device, 4) < 2, two_ref[...].astype(F32), far_ref[...].astype(F32))
    xn = jnp.concatenate([normalize(e)[0].astype(BF) for e in (l1, l2)], axis=0)
    qn_ref[...] = jax.nn.silu(dot(xn, w_ref[:, width:2 * width])).astype(BF)
    ends = history_ends(lengths_ref, first_row, (8, rows))[0:1]
    row = lax.broadcasted_iota(jnp.int32, (later, rows), 0)
    share = jnp.where(row + (first_row + rows) < ends, 1.0 / EV_DEV, 0.0)
    for h in range(heads):
        c = slice(h * hd, (h + 1) * hd)
        act, slope = silu_and_slope(dot_nt(qn_ref[:, c], k_ref[:, c]) * scale)
        wn_ref[:, c] = (act * share).astype(BF)
        sn_ref[:, c] = (slope * share).astype(BF)


def middle_kernel(
    q_ref, k_ref, v_ref, kh_ref, vh_ref, wt_ref, sl_ref, gm_ref, sq_ref, gpu_ref, w_ref,
    dk_ref, dv_ref, gx_ref, *, heads, scale,
):
    width = q_ref.shape[1]
    early = kh_ref.shape[0]
    hd = width // heads
    grad_q = []
    for h in range(heads):
        c = slice(h * hd, (h + 1) * hd)
        gm = gm_ref[:, c]
        key = jnp.concatenate([kh_ref[:, c], k_ref[:, c]], axis=0)
        val = jnp.concatenate([vh_ref[:, c], v_ref[:, c]], axis=0)
        ds = (dot_nt(gm, val) * sl_ref[h].astype(F32)).astype(BF)
        grad_q.append((dot(ds, key) * scale * sq_ref[:, c].astype(F32)).astype(BF))
        dk_ref[:, c] = dot_tn(ds[:, early:], q_ref[:, c])
        dv_ref[:, c] = dot_tn(wt_ref[h][:, early:], gm)
    gpq = jnp.concatenate(grad_q, axis=1)
    gx_ref[...] = dot_nt(gpu_ref[...], w_ref[:, :width]) + dot_nt(gpq, w_ref[:, width:2 * width])


def last_kernel(
    ev_ref, g1_ref, g2_ref, qn_ref, wn_ref, sn_ref, k_ref, v_ref, dk_ref, dv_ref,
    sk_ref, sv_ref, w_ref, gx_ref, gout_ref, out_ref, *, heads, scale,
):
    width = ev_ref.shape[1]
    hd = width // heads
    grad_k, grad_v = [], []
    for h in range(heads):
        c = slice(h * hd, (h + 1) * hd)
        gm = jnp.concatenate([g1_ref[:, c], g2_ref[:, c]], axis=0)
        ds = (dot_nt(gm, v_ref[:, c]) * sn_ref[:, c].astype(F32)).astype(BF)
        gk = (dk_ref[:, c] + dot_tn(ds, qn_ref[:, c])) * scale
        gv = dv_ref[:, c] + dot_tn(wn_ref[:, c], gm)
        grad_k.append((gk * sk_ref[:, c].astype(F32)).astype(BF))
        grad_v.append((gv * sv_ref[:, c].astype(F32)).astype(BF))
    grad_x = (
        gx_ref[...]
        + dot_nt(jnp.concatenate(grad_k, axis=1), w_ref[:, 2 * width:3 * width])
        + dot_nt(jnp.concatenate(grad_v, axis=1), w_ref[:, 3 * width:])
    )
    normed_x, inv_x = normalize(ev_ref[...].astype(F32))
    out_ref[...] = norm_back(grad_x, normed_x, inv_x) + gout_ref[...]


def call(kernel, outs, flops, *args, scalars=False, scratch=()):
    vmem = pl.BlockSpec(memory_space=pltpu.VMEM)
    specs = [vmem] * len(args)
    if scalars:
        specs[0] = pl.BlockSpec(memory_space=pltpu.SMEM)
    return pl.pallas_call(
        kernel,
        in_specs=specs,
        out_specs=[vmem] * len(outs),
        out_shape=list(outs),
        scratch_shapes=list(scratch),
        cost_estimate=cost(flops, *args, *outs),
        compiler_params=pltpu.CompilerParams(vmem_limit_bytes=VMEM_BYTES),
    )(*args)


def shaped(shape, dtype):
    return jax.ShapeDtypeStruct(shape, dtype)


def cost(flops, *arrays):
    return pl.CostEstimate(
        flops=flops,
        bytes_accessed=sum(math.prod(x.shape) * x.dtype.itemsize for x in arrays),
        transcendentals=0,
    )


def layer(events, input_weight, output_weight, positives, negatives, log_probs, lengths):
    rows, width = events.shape
    hd = width // HEADS
    scale = 1.0 / math.sqrt(hd)
    early = REACH * rows
    keys = early + rows
    low_block = shaped((rows, width), BF)
    wide_block = shaped((rows, width), F32)

    dp_n, seq_n = lax.axis_size("dp"), lax.axis_size("seq")
    plane_n = dp_n * seq_n
    half = plane_n // 2
    paired = width % (plane_n * 128) == 0 and is_pow2(half) and half > 0
    sent = width // 2 if paired else 0

    near = neighbours(events)
    part = negatives.shape[0] // plane_n
    if part % 16 == 0:
        piece, = call(
            piece_kernel, [shaped((part, width + 128), BF)], 0,
            negatives, log_probs[None, :],
        )
    else:
        at = lax.axis_index(PLANE) * part
        raw = lax.dynamic_slice_in_dim(negatives, at, part, 0).astype(F32)
        unit = raw * lax.rsqrt(jnp.sum(raw * raw, axis=1, keepdims=True))
        logs = lax.dynamic_slice_in_dim(log_probs, at, part, 0)
        piece = jnp.concatenate(
            [unit.astype(BF), jnp.broadcast_to(logs[:, None], (part, 128))], axis=1
        )
    neg0, neg1 = gathered(piece)

    flops = 2 * rows * width * width
    up, q, k, v, s_up, s_q, s_k, s_v = call(
        own_kernel, [low_block] * 8, 4 * flops, events, input_weight
    )

    early_block = shaped((early, width), BF)
    head_block = shaped((HEADS, rows, keys), BF)
    kh, vh, wts, slopes, mixed = call(
        functools.partial(attend_kernel, heads=HEADS, scale=scale),
        [early_block, early_block, head_block, head_block, wide_block], 5 * flops,
        lengths, *near, q, k, v, input_weight, scalars=True,
    )
    mine, pay, grad_out, gpu, gm = call(
        functools.partial(loss_kernel, plane_cols=plane_n if paired else 0),
        [
            shaped((rows, sent or width), BF), shaped((rows, sent + width), BF),
            wide_block, low_block, low_block,
        ],
        4 * flops, mixed, events, positives, neg0, neg1, s_up, up, output_weight,
        scratch=[pltpu.VMEM((rows, width), BF)],
    )

    if paired:
        got = swapped(pay, "dp", 1)
        own_sum, *sends = call(
            product_kernel,
            [shaped((width // plane_n, width), F32)]
            + [shaped((width // plane_n, width), BF)] * (half - 1),
            flops, mine, pay, got,
        )
        total = own_sum
        for j in range(1, half):
            pairs = []
            for i in range(plane_n):
                d, s = divmod(i, seq_n)
                t = ((d // 2) * seq_n + s) ^ j
                pairs.append((i, ((t // seq_n) * 2 + d % 2) * seq_n + t % seq_n))
            total = total + lax.ppermute(sends[j - 1], PLANE, pairs).astype(F32)
    else:
        total = lax.psum_scatter(dot_tn(mine, pay), PLANE, scatter_dimension=0, tiled=True)

    g2 = shifted(gm, -2)
    g1 = shifted(gm, -1)

    qn, wn, sn = call(
        functools.partial(later_kernel, heads=HEADS, scale=scale),
        [early_block] * 3, 3 * flops, lengths, *near, k, input_weight, scalars=True,
    )
    dk, dv, gx = call(
        functools.partial(middle_kernel, heads=HEADS, scale=scale),
        [wide_block] * 3, 4 * flops,
        q, k, v, kh, vh, wts, slopes, gm, s_q, gpu, input_weight,
    )

    pool_n = lax.axis_size("pool")
    if is_pow2(pool_n) and pool_n > 2:
        mid = total.shape[0] // 2
        odd = lax.rem(lax.axis_index("pool"), 2) == 1
        lower, upper = total[:mid], total[mid:]
        kept = jnp.where(odd, upper, lower)
        kept = kept + swapped(jnp.where(odd, lower, upper).astype(BF), "pool", 1).astype(F32)
        for b in range(1, pool_n.bit_length() - 1):
            low = kept.astype(BF)
            kept = low.astype(F32) + swapped(low, "pool", 1 << b).astype(F32)
        low = kept.astype(BF)
        other = swapped(low, "pool", 1)
        total = jnp.concatenate(
            [jnp.where(odd, other, low), jnp.where(odd, low, other)], axis=0
        ).astype(F32)
    else:
        total = lax.psum(total, "pool")

    d_events, = call(
        functools.partial(last_kernel, heads=HEADS, scale=scale),
        [wide_block], 4 * flops,
        events, g1, g2, qn, wn, sn, k, v, dk, dv, s_k, s_v, input_weight, gx, grad_out,
    )
    return (d_events, total)


def solution(mesh):
    placed = (
        P(("dp", "seq", "pool"), None),
        P(),
        P(),
        P(("dp", "seq", "pool"), None),
        P("pool", None),
        P("pool"),
        P(),
    )
    return jax.shard_map(
        layer,
        mesh=mesh,
        in_specs=placed,
        out_specs=(P(("dp", "seq", "pool"), None), P(("dp", "seq"), None)),
        check_vma=False,
    )
```

```python
import functools
import math

import jax
import jax.numpy as jnp
from jax import lax
from jax.experimental import pallas as pl
from jax.experimental.pallas import tpu as pltpu
from jax.sharding import PartitionSpec as P


HEADS = 8
EV_DEV = 128
REACH = 2

epsilon = 1e-05
sharpness_divisor = 0.05
loss_multiplier = 8.0

ALL = ("dp", "seq", "pool")
PLANE = ("dp", "seq")
VMEM_BYTES = 16 << 20
BF = jnp.bfloat16
F32 = jnp.float32

NT = (((1,), (1,)), ((), ()))
TN = (((0,), (0,)), ((), ()))


def dot(a, b):
    return jnp.dot(a, b, preferred_element_type=F32)


def dot_nt(a, b):
    return lax.dot_general(a, b, NT, preferred_element_type=F32)


def dot_tn(a, b):
    return lax.dot_general(a, b, TN, preferred_element_type=F32)


def shifted(x, by):
    length = lax.axis_size(ALL)
    pairs = [(i, i + by) for i in range(length) if 0 <= i + by < length]
    return lax.ppermute(x, ALL, pairs)


def neighbours(x):
    n = lax.axis_size(ALL)
    two = lax.ppermute(x, ALL, [(i, i ^ 2) for i in range(n)])
    odd = [(i, i + 1) for i in range(1, n - 1, 2)]
    cross = lax.ppermute(x, ALL, odd + [(j, i) for i, j in odd])
    one = lax.ppermute(x, ALL, [(i, i ^ 1) for i in range(n)])
    if lax.axis_size("pool") == 4:
        source, by = two, 4
    else:
        source, by = x, -2
    pairs = [(i, i + by if i % 4 < 2 else i - by) for i in range(n)]
    far = lax.ppermute(source, ALL, [(i, j) for i, j in pairs if 0 <= j < n])
    return one, cross, two, far


def is_pow2(n):
    return n & (n - 1) == 0


def swapped(x, axis, bit):
    return lax.ppermute(x, axis, [(i, i ^ bit) for i in range(lax.axis_size(axis))])


def gather_stages(sizes):
    stages = []
    for axis in PLANE[::-1]:
        stages += [(axis, 1 << b) for b in reversed(range(sizes[axis].bit_length() - 1))]
    return stages


def gathered(x):
    sizes = {axis: lax.axis_size(axis) for axis in ALL}
    if all(is_pow2(n) for n in sizes.values()):
        parts = [x] + [swapped(x, "pool", k) for k in range(1, sizes["pool"])]
        for axis, bit in gather_stages(sizes):
            x = jnp.concatenate(parts, axis=0)
            parts = [x, swapped(x, axis, bit)]
        return parts
    for axis, n in sizes.items():
        turns = [lax.ppermute(x, axis, [(i, (i + k) % n) for i in range(n)]) for k in range(1, n)]
        x = jnp.concatenate([x] + turns, axis=0)
    return [x[:x.shape[0] // 2], x[x.shape[0] // 2:]]


def normalize(row_data):
    centred = row_data - jnp.mean(row_data, axis=1, keepdims=True)
    inv_std = lax.rsqrt(jnp.mean(centred * centred, axis=1, keepdims=True) + epsilon)
    return centred * inv_std, inv_std


def norm_back(grad_in, normed, inv_std):
    return (
        grad_in
        - jnp.mean(grad_in, axis=1, keepdims=True)
        - normed * jnp.mean(grad_in * normed, axis=1, keepdims=True)
    ) * inv_std


def silu_and_slope(v):
    sig = jax.nn.sigmoid(v)
    return v * sig, sig * (1.0 + v * (1.0 - sig))


def own_kernel(x_ref, w_ref, *out_refs):
    width = x_ref.shape[1]
    parts = len(out_refs) // 2
    xn = normalize(x_ref[...].astype(F32))[0].astype(BF)
    for i in range(parts):
        act, slope = silu_and_slope(dot(xn, w_ref[:, i * width:(i + 1) * width]))
        out_refs[i][...] = act.astype(BF)
        out_refs[parts + i][...] = slope.astype(BF)


def history_ends(lengths_ref, first, shape):
    column = first + lax.broadcasted_iota(jnp.int32, shape, 1)
    far = jnp.full(shape, jnp.iinfo(jnp.int32).max, jnp.int32)

    def body(u, carry):
        end, found = carry
        end = end + lengths_ref[u]
        return end, jnp.minimum(found, jnp.where(end > column, end, far))

    found = lax.fori_loop(0, lengths_ref.shape[0], body, (jnp.int32(0), far))[1]
    return jnp.where(column >= 0, found, 0)


def piece_kernel(neg_ref, log_ref, out_ref):
    part = out_ref.shape[0]
    width = neg_ref.shape[1]
    at = pl.multiple_of(lax.axis_index(PLANE) * part, part)
    raw = neg_ref[pl.ds(at, part), :].astype(F32)
    out_ref[:, :width] = (
        raw * lax.rsqrt(jnp.sum(raw * raw, axis=1, keepdims=True))
    ).astype(BF)
    logs = log_ref[...].astype(F32)
    shape = (part, logs.shape[1])
    wanted = lax.broadcasted_iota(jnp.int32, shape, 1) == at + lax.broadcasted_iota(
        jnp.int32, shape, 0
    )
    mine = jnp.sum(jnp.where(wanted, logs, 0.0), axis=1, keepdims=True)
    out_ref[:, width:] = jnp.broadcast_to(mine, (part, 128)).astype(BF)


def attend_kernel(
    lengths_ref, one_ref, cross_ref, two_ref, far_ref, q_ref, k_ref, v_ref, w_ref,
    kh_ref, vh_ref, wt_ref, sl_ref, mixed_ref, *, heads, scale,
):
    rows, width = q_ref.shape
    early = kh_ref.shape[0]
    keys = early + rows
    hd = width // heads
    device = lax.axis_index(ALL)
    first_row = device * rows
    e2 = jnp.where(lax.rem(device, 4) < 2, far_ref[...].astype(F32), two_ref[...].astype(F32))
    e1 = jnp.where(lax.rem(device, 2) == 1, one_ref[...].astype(F32), cross_ref[...].astype(F32))
    xn = jnp.concatenate([normalize(e)[0].astype(BF) for e in (e2, e1)], axis=0)
    kh_ref[...] = jax.nn.silu(dot(xn, w_ref[:, 2 * width:3 * width])).astype(BF)
    vh_ref[...] = jax.nn.silu(dot(xn, w_ref[:, 3 * width:])).astype(BF)
    ends = history_ends(lengths_ref, first_row - early, (8, keys))[0:1]
    col = lax.broadcasted_iota(jnp.int32, (rows, keys), 1)
    row = lax.broadcasted_iota(jnp.int32, (rows, keys), 0)
    allowed = (row + first_row < ends) & (col <= row + early)
    share = jnp.where(allowed, 1.0 / EV_DEV, 0.0)
    for h in range(heads):
        c = slice(h * hd, (h + 1) * hd)
        key = jnp.concatenate([kh_ref[:, c], k_ref[:, c]], axis=0)
        val = jnp.concatenate([vh_ref[:, c], v_ref[:, c]], axis=0)
        act, slope = silu_and_slope(dot_nt(q_ref[:, c], key) * scale)
        wts = (act * share).astype(BF)
        wt_ref[h] = wts
        sl_ref[h] = (slope * share).astype(BF)
        mixed_ref[:, c] = dot(wts, val)


def loss_kernel(
    mixed_ref, ev_ref, pos_ref, neg0_ref, neg1_ref, su_ref, up_ref, wo_ref,
    mine_ref, pay_ref, gout_ref, gpu_ref, gm_ref, gated_ref, *, plane_cols,
):
    rows, width = ev_ref.shape
    event_rows = ev_ref[...].astype(F32)
    normed_o, inv_o = normalize(mixed_ref[...])
    update = up_ref[...].astype(F32)
    gated = (normed_o * update).astype(BF)
    gated_ref[...] = gated
    dp_i, seq_n = lax.axis_index("dp"), lax.axis_size("seq")
    core = lax.rem(dp_i, 2)
    group = (dp_i // 2) * seq_n + lax.axis_index("seq")
    half = plane_cols // 2
    per = width // plane_cols if half else 0
    if not half:
        mine_ref[...] = gated
    for j in range(half):
        g = group ^ j
        base = (g // seq_n) * 2 * seq_n + lax.rem(g, seq_n)
        a0 = pl.multiple_of((base + core * seq_n) * per, per)
        a1 = pl.multiple_of((base + (1 - core) * seq_n) * per, per)
        mine_ref[:, j * per:(j + 1) * per] = gated_ref[:, pl.ds(a0, per)]
        pay_ref[:, j * per:(j + 1) * per] = gated_ref[:, pl.ds(a1, per)]
    layer_out = dot(gated, wo_ref[...]) + event_rows
    inv_norm = lax.rsqrt(jnp.sum(layer_out * layer_out, axis=1, keepdims=True))
    unit = layer_out * inv_norm
    positive = pos_ref[...].astype(F32)
    target = positive * lax.rsqrt(jnp.sum(positive * positive, axis=1, keepdims=True))
    pos_logit = jnp.sum(unit * target, axis=1, keepdims=True) / sharpness_divisor
    neg = jnp.concatenate([neg0_ref[:, :width], neg1_ref[:, :width]], axis=0)
    logs = jnp.concatenate([neg0_ref[:, width:], neg1_ref[:, width:]], axis=0)
    lane = lax.broadcasted_iota(jnp.int32, (rows, logs.shape[1]), 1)
    offset = dot_nt(jnp.where(lane == 0, 1.0, 0.0).astype(BF), logs)
    neg_logit = dot_nt(unit.astype(BF), neg) / sharpness_divisor - offset
    exp_terms = jnp.exp(neg_logit)
    pos_exp = jnp.exp(pos_logit)
    total = pos_exp + jnp.sum(exp_terms, axis=1, keepdims=True)
    weighted = dot(exp_terms.astype(BF), neg)
    grad_unit = (loss_multiplier / sharpness_divisor) * (
        weighted / total + (pos_exp / total - 1.0) * target
    )
    grad_out = (grad_unit - unit * jnp.sum(unit * grad_unit, axis=1, keepdims=True)) * inv_norm
    gout_ref[...] = grad_out
    low = grad_out.astype(BF)
    pay_ref[:, half * per:] = low
    grad_gated = dot_nt(low, wo_ref[...])
    gpu_ref[...] = (grad_gated * normed_o * su_ref[...].astype(F32)).astype(BF)
    gm_ref[...] = norm_back(grad_gated * update, normed_o, inv_o).astype(BF)


def product_kernel(mine_ref, pay_ref, got_ref, own_ref, *send_refs):
    cols = mine_ref.shape[1]
    per = cols // (len(send_refs) + 1)
    low = jnp.concatenate([pay_ref[:, cols:], got_ref[:, cols:]], axis=0)
    gated = jnp.concatenate([mine_ref[...], got_ref[:, :cols]], axis=0)
    out = dot_tn(gated, low)
    own_ref[...] = out[:per]
    for j, send_ref in enumerate(send_refs, 1):
        send_ref[...] = out[j * per:(j + 1) * per].astype(BF)


def sum_kernel(own_ref, *refs):
    *got_refs, kept_ref, give_ref = refs
    mid = kept_ref.shape[0]
    odd = lax.rem(lax.axis_index("pool"), 2) == 1
    total = own_ref[...]
    for got_ref in got_refs:
        total = total + got_ref[...].astype(F32)
    lower, upper = total[:mid], total[mid:]
    kept_ref[...] = jnp.where(odd, upper, lower)
    give_ref[...] = jnp.where(odd, lower, upper).astype(BF)


def join_kernel(kept_ref, got_ref, out_ref):
    mid = kept_ref.shape[0]
    odd = lax.rem(lax.axis_index("pool"), 2) == 1
    kept, got = kept_ref[...].astype(F32), got_ref[...].astype(F32)
    out_ref[:mid] = jnp.where(odd, got, kept)
    out_ref[mid:] = jnp.where(odd, kept, got)


def later_kernel(
    lengths_ref, one_ref, cross_ref, two_ref, far_ref, k_ref, w_ref,
    qn_ref, wn_ref, sn_ref, *, heads, scale,
):
    rows, width = k_ref.shape
    later = wn_ref.shape[0]
    hd = width // heads
    device = lax.axis_index(ALL)
    first_row = device * rows
    l1 = jnp.where(lax.rem(device, 2) == 1, cross_ref[...].astype(F32), one_ref[...].astype(F32))
    l2 = jnp.where(lax.rem(device, 4) < 2, two_ref[...].astype(F32), far_ref[...].astype(F32))
    xn = jnp.concatenate([normalize(e)[0].astype(BF) for e in (l1, l2)], axis=0)
    qn_ref[...] = jax.nn.silu(dot(xn, w_ref[:, width:2 * width])).astype(BF)
    ends = history_ends(lengths_ref, first_row, (8, rows))[0:1]
    row = lax.broadcasted_iota(jnp.int32, (later, rows), 0)
    share = jnp.where(row + (first_row + rows) < ends, 1.0 / EV_DEV, 0.0)
    for h in range(heads):
        c = slice(h * hd, (h + 1) * hd)
        act, slope = silu_and_slope(dot_nt(qn_ref[:, c], k_ref[:, c]) * scale)
        wn_ref[:, c] = (act * share).astype(BF)
        sn_ref[:, c] = (slope * share).astype(BF)


def middle_kernel(
    q_ref, k_ref, v_ref, kh_ref, vh_ref, wt_ref, sl_ref, gm_ref, sq_ref, gpu_ref, w_ref,
    dk_ref, dv_ref, gx_ref, *, heads, scale,
):
    width = q_ref.shape[1]
    early = kh_ref.shape[0]
    hd = width // heads
    grad_q = []
    for h in range(heads):
        c = slice(h * hd, (h + 1) * hd)
        gm = gm_ref[:, c]
        key = jnp.concatenate([kh_ref[:, c], k_ref[:, c]], axis=0)
        val = jnp.concatenate([vh_ref[:, c], v_ref[:, c]], axis=0)
        ds = (dot_nt(gm, val) * sl_ref[h].astype(F32)).astype(BF)
        grad_q.append((dot(ds, key) * scale * sq_ref[:, c].astype(F32)).astype(BF))
        dk_ref[:, c] = dot_tn(ds[:, early:], q_ref[:, c])
        dv_ref[:, c] = dot_tn(wt_ref[h][:, early:], gm)
    gpq = jnp.concatenate(grad_q, axis=1)
    gx_ref[...] = dot_nt(gpu_ref[...], w_ref[:, :width]) + dot_nt(gpq, w_ref[:, width:2 * width])


def last_kernel(
    ev_ref, g1_ref, g2_ref, qn_ref, wn_ref, sn_ref, k_ref, v_ref, dk_ref, dv_ref,
    sk_ref, sv_ref, w_ref, gx_ref, gout_ref, out_ref, *, heads, scale,
):
    width = ev_ref.shape[1]
    hd = width // heads
    grad_k, grad_v = [], []
    for h in range(heads):
        c = slice(h * hd, (h + 1) * hd)
        gm = jnp.concatenate([g1_ref[:, c], g2_ref[:, c]], axis=0)
        ds = (dot_nt(gm, v_ref[:, c]) * sn_ref[:, c].astype(F32)).astype(BF)
        gk = (dk_ref[:, c] + dot_tn(ds, qn_ref[:, c])) * scale
        gv = dv_ref[:, c] + dot_tn(wn_ref[:, c], gm)
        grad_k.append((gk * sk_ref[:, c].astype(F32)).astype(BF))
        grad_v.append((gv * sv_ref[:, c].astype(F32)).astype(BF))
    grad_x = (
        gx_ref[...]
        + dot_nt(jnp.concatenate(grad_k, axis=1), w_ref[:, 2 * width:3 * width])
        + dot_nt(jnp.concatenate(grad_v, axis=1), w_ref[:, 3 * width:])
    )
    normed_x, inv_x = normalize(ev_ref[...].astype(F32))
    out_ref[...] = norm_back(grad_x, normed_x, inv_x) + gout_ref[...]


def call(kernel, outs, flops, *args, scalars=False, scratch=(), far=()):
    vmem = pl.BlockSpec(memory_space=pltpu.VMEM)
    specs = [vmem] * len(args)
    if scalars:
        specs[0] = pl.BlockSpec(memory_space=pltpu.SMEM)
    for i in far:
        specs[i] = pl.BlockSpec(memory_space=pltpu.HBM)
    return pl.pallas_call(
        kernel,
        in_specs=specs,
        out_specs=[vmem] * len(outs),
        out_shape=list(outs),
        scratch_shapes=list(scratch),
        cost_estimate=cost(flops, *args, *outs),
        compiler_params=pltpu.CompilerParams(vmem_limit_bytes=VMEM_BYTES),
    )(*args)


def shaped(shape, dtype):
    return jax.ShapeDtypeStruct(shape, dtype)


def cost(flops, *arrays):
    return pl.CostEstimate(
        flops=flops,
        bytes_accessed=sum(math.prod(x.shape) * x.dtype.itemsize for x in arrays),
        transcendentals=0,
    )


def layer(events, input_weight, output_weight, positives, negatives, log_probs, lengths):
    rows, width = events.shape
    hd = width // HEADS
    scale = 1.0 / math.sqrt(hd)
    early = REACH * rows
    keys = early + rows
    low_block = shaped((rows, width), BF)
    wide_block = shaped((rows, width), F32)

    dp_n, seq_n = lax.axis_size("dp"), lax.axis_size("seq")
    plane_n = dp_n * seq_n
    half = plane_n // 2
    paired = width % (plane_n * 128) == 0 and is_pow2(half) and half > 0
    sent = width // 2 if paired else 0

    near = neighbours(events)
    part = negatives.shape[0] // plane_n
    if part % 16 == 0:
        piece, = call(
            piece_kernel, [shaped((part, width + 128), BF)], 0,
            negatives, log_probs[None, :],
        )
    else:
        at = lax.axis_index(PLANE) * part
        raw = lax.dynamic_slice_in_dim(negatives, at, part, 0).astype(F32)
        unit = raw * lax.rsqrt(jnp.sum(raw * raw, axis=1, keepdims=True))
        logs = lax.dynamic_slice_in_dim(log_probs, at, part, 0)
        piece = jnp.concatenate(
            [unit.astype(BF), jnp.broadcast_to(logs[:, None], (part, 128))], axis=1
        )
    neg0, neg1 = gathered(piece)

    flops = 2 * rows * width * width
    up, q, k, v, s_up, s_q, s_k, s_v = call(
        own_kernel, [low_block] * 8, 4 * flops, events, input_weight
    )
    weight = input_weight

    early_block = shaped((early, width), BF)
    head_block = shaped((HEADS, rows, keys), BF)
    kh, vh, wts, slopes, mixed = call(
        functools.partial(attend_kernel, heads=HEADS, scale=scale),
        [early_block, early_block, head_block, head_block, wide_block], 5 * flops,
        lengths, *near, q, k, v, weight, scalars=True,
    )
    mine, pay, grad_out, gpu, gm = call(
        functools.partial(loss_kernel, plane_cols=plane_n if paired else 0),
        [
            shaped((rows, sent or width), BF), shaped((rows, sent + width), BF),
            wide_block, low_block, low_block,
        ],
        4 * flops, mixed, events, positives, neg0, neg1, s_up, up, output_weight,
        scratch=[pltpu.VMEM((rows, width), BF)],
    )

    if paired:
        got = swapped(pay, "dp", 1)
        own_sum, *sends = call(
            product_kernel,
            [shaped((width // plane_n, width), F32)]
            + [shaped((width // plane_n, width), BF)] * (half - 1),
            flops, mine, pay, got,
        )
        terms = [own_sum]
        for j in range(1, half):
            pairs = []
            for i in range(plane_n):
                d, s = divmod(i, seq_n)
                t = ((d // 2) * seq_n + s) ^ j
                pairs.append((i, ((t // seq_n) * 2 + d % 2) * seq_n + t % seq_n))
            terms.append(lax.ppermute(sends[j - 1], PLANE, pairs))
    else:
        terms = [lax.psum_scatter(dot_tn(mine, pay), PLANE, scatter_dimension=0, tiled=True)]

    g2 = shifted(gm, -2)
    g1 = shifted(gm, -1)

    qn, wn, sn = call(
        functools.partial(later_kernel, heads=HEADS, scale=scale),
        [early_block] * 3, 3 * flops, lengths, *near, k, weight, scalars=True,
    )
    dk, dv, gx = call(
        functools.partial(middle_kernel, heads=HEADS, scale=scale),
        [wide_block] * 3, 4 * flops,
        q, k, v, kh, vh, wts, slopes, gm, s_q, gpu, weight,
    )

    pool_n = lax.axis_size("pool")
    if is_pow2(pool_n) and pool_n > 2:
        rows_out = terms[0].shape[0]
        kept, give = call(
            sum_kernel,
            [shaped((rows_out // 2, width), F32), shaped((rows_out // 2, width), BF)], 0, *terms,
        )
        kept = kept + swapped(give, "pool", 1).astype(F32)
        for b in range(1, pool_n.bit_length() - 1):
            low = kept.astype(BF)
            kept = low.astype(F32) + swapped(low, "pool", 1 << b).astype(F32)
        low = kept.astype(BF)
        other = swapped(low, "pool", 1)
        total, = call(join_kernel, [shaped((rows_out, width), F32)], 0, low, other)
    else:
        total = lax.psum(sum(t.astype(F32) for t in terms), "pool")

    d_events, = call(
        functools.partial(last_kernel, heads=HEADS, scale=scale),
        [wide_block], 4 * flops,
        events, g1, g2, qn, wn, sn, k, v, dk, dv, s_k, s_v, weight, gx, grad_out,
    )
    return (d_events, total)


def solution(mesh):
    placed = (
        P(("dp", "seq", "pool"), None),
        P(),
        P(),
        P(("dp", "seq", "pool"), None),
        P("pool", None),
        P("pool"),
        P(),
    )
    return jax.shard_map(
        layer,
        mesh=mesh,
        in_specs=placed,
        out_specs=(P(("dp", "seq", "pool"), None), P(("dp", "seq"), None)),
        check_vma=False,
    )
```

```python
import functools
import math

import jax
import jax.numpy as jnp
from jax import lax
from jax.experimental import pallas as pl
from jax.experimental.pallas import tpu as pltpu
from jax.sharding import PartitionSpec as P


HEADS = 8
EV_DEV = 128
REACH = 2

epsilon = 1e-05
sharpness_divisor = 0.05
loss_multiplier = 8.0

ALL = ("dp", "seq", "pool")
PLANE = ("dp", "seq")
VMEM_BYTES = 16 << 20
BF = jnp.bfloat16
F32 = jnp.float32

NT = (((1,), (1,)), ((), ()))
TN = (((0,), (0,)), ((), ()))


def dot(a, b):
    return jnp.dot(a, b, preferred_element_type=F32)


def dot_nt(a, b):
    return lax.dot_general(a, b, NT, preferred_element_type=F32)


def dot_tn(a, b):
    return lax.dot_general(a, b, TN, preferred_element_type=F32)


def shifted(x, by):
    length = lax.axis_size(ALL)
    pairs = [(i, i + by) for i in range(length) if 0 <= i + by < length]
    return lax.ppermute(x, ALL, pairs)


def neighbours(x):
    n = lax.axis_size(ALL)
    two = lax.ppermute(x, ALL, [(i, i ^ 2) for i in range(n)])
    odd = [(i, i + 1) for i in range(1, n - 1, 2)]
    cross = lax.ppermute(x, ALL, odd + [(j, i) for i, j in odd])
    one = lax.ppermute(x, ALL, [(i, i ^ 1) for i in range(n)])
    if lax.axis_size("pool") == 4:
        source, by = two, 4
    else:
        source, by = x, -2
    pairs = [(i, i + by if i % 4 < 2 else i - by) for i in range(n)]
    far = lax.ppermute(source, ALL, [(i, j) for i, j in pairs if 0 <= j < n])
    return one, cross, two, far


def two_later(x):
    if lax.axis_size("pool") != 4:
        moved = shifted(x, -2)
        return moved, moved
    n = lax.axis_size(ALL)
    two = lax.ppermute(x, ALL, [(i, i ^ 2) for i in range(n)])
    return two, lax.ppermute(two, ALL, [(i, i - 4) for i in range(4, n) if i % 4 >= 2])


def is_pow2(n):
    return n & (n - 1) == 0


def swapped(x, axis, bit):
    return lax.ppermute(x, axis, [(i, i ^ bit) for i in range(lax.axis_size(axis))])


def gather_stages(sizes):
    stages = []
    for axis in PLANE[::-1]:
        stages += [(axis, 1 << b) for b in reversed(range(sizes[axis].bit_length() - 1))]
    return stages


def gathered(x):
    sizes = {axis: lax.axis_size(axis) for axis in ALL}
    if all(is_pow2(n) for n in sizes.values()):
        parts = [x] + [swapped(x, "pool", k) for k in range(1, sizes["pool"])]
        for axis, bit in gather_stages(sizes):
            x = jnp.concatenate(parts, axis=0)
            parts = [x, swapped(x, axis, bit)]
        return parts
    for axis, n in sizes.items():
        turns = [lax.ppermute(x, axis, [(i, (i + k) % n) for i in range(n)]) for k in range(1, n)]
        x = jnp.concatenate([x] + turns, axis=0)
    return [x[:x.shape[0] // 2], x[x.shape[0] // 2:]]


def normalize(row_data):
    centred = row_data - jnp.mean(row_data, axis=1, keepdims=True)
    inv_std = lax.rsqrt(jnp.mean(centred * centred, axis=1, keepdims=True) + epsilon)
    return centred * inv_std, inv_std


def norm_back(grad_in, normed, inv_std):
    return (
        grad_in
        - jnp.mean(grad_in, axis=1, keepdims=True)
        - normed * jnp.mean(grad_in * normed, axis=1, keepdims=True)
    ) * inv_std


def silu_and_slope(v):
    sig = jax.nn.sigmoid(v)
    return v * sig, sig * (1.0 + v * (1.0 - sig))


def own_kernel(x_ref, w_ref, *out_refs):
    width = x_ref.shape[1]
    parts = len(out_refs) // 2
    xn = normalize(x_ref[...].astype(F32))[0].astype(BF)
    for i in range(parts):
        act, slope = silu_and_slope(dot(xn, w_ref[:, i * width:(i + 1) * width]))
        out_refs[i][...] = act.astype(BF)
        out_refs[parts + i][...] = slope.astype(BF)


def history_ends(lengths_ref, first, shape):
    column = first + lax.broadcasted_iota(jnp.int32, shape, 1)
    far = jnp.full(shape, jnp.iinfo(jnp.int32).max, jnp.int32)

    def body(u, carry):
        end, found = carry
        end = end + lengths_ref[u]
        return end, jnp.minimum(found, jnp.where(end > column, end, far))

    found = lax.fori_loop(0, lengths_ref.shape[0], body, (jnp.int32(0), far))[1]
    return jnp.where(column >= 0, found, 0)


def piece_kernel(neg_ref, log_ref, out_ref):
    part = out_ref.shape[0]
    width = neg_ref.shape[1]
    at = pl.multiple_of(lax.axis_index(PLANE) * part, part)
    raw = neg_ref[pl.ds(at, part), :].astype(F32)
    out_ref[:, :width] = (
        raw * lax.rsqrt(jnp.sum(raw * raw, axis=1, keepdims=True))
    ).astype(BF)
    logs = log_ref[...].astype(F32)
    shape = (part, logs.shape[1])
    wanted = lax.broadcasted_iota(jnp.int32, shape, 1) == at + lax.broadcasted_iota(
        jnp.int32, shape, 0
    )
    mine = jnp.sum(jnp.where(wanted, logs, 0.0), axis=1, keepdims=True)
    out_ref[:, width:] = jnp.broadcast_to(mine, (part, 128)).astype(BF)


def attend_kernel(
    lengths_ref, one_ref, cross_ref, two_ref, far_ref, q_ref, k_ref, v_ref, w_ref,
    kh_ref, vh_ref, wt_ref, sl_ref, mixed_ref, *, heads, scale,
):
    rows, width = q_ref.shape
    early = kh_ref.shape[0]
    keys = early + rows
    hd = width // heads
    device = lax.axis_index(ALL)
    first_row = device * rows
    e2 = jnp.where(lax.rem(device, 4) < 2, far_ref[...].astype(F32), two_ref[...].astype(F32))
    e1 = jnp.where(lax.rem(device, 2) == 1, one_ref[...].astype(F32), cross_ref[...].astype(F32))
    xn = jnp.concatenate([normalize(e)[0].astype(BF) for e in (e2, e1)], axis=0)
    kh_ref[...] = jax.nn.silu(dot(xn, w_ref[:, 2 * width:3 * width])).astype(BF)
    vh_ref[...] = jax.nn.silu(dot(xn, w_ref[:, 3 * width:])).astype(BF)
    ends = history_ends(lengths_ref, first_row - early, (8, keys))[0:1]
    col = lax.broadcasted_iota(jnp.int32, (rows, keys), 1)
    row = lax.broadcasted_iota(jnp.int32, (rows, keys), 0)
    allowed = (row + first_row < ends) & (col <= row + early)
    share = jnp.where(allowed, 1.0 / EV_DEV, 0.0)
    for h in range(heads):
        c = slice(h * hd, (h + 1) * hd)
        key = jnp.concatenate([kh_ref[:, c], k_ref[:, c]], axis=0)
        val = jnp.concatenate([vh_ref[:, c], v_ref[:, c]], axis=0)
        act, slope = silu_and_slope(dot_nt(q_ref[:, c], key) * scale)
        wts = (act * share).astype(BF)
        wt_ref[h] = wts
        sl_ref[h] = (slope * share).astype(BF)
        mixed_ref[:, c] = dot(wts, val)


def loss_kernel(
    mixed_ref, ev_ref, pos_ref, neg0_ref, neg1_ref, su_ref, up_ref, wo_ref,
    mine_ref, pay_ref, gout_ref, gpu_ref, gm_ref, gated_ref, *, plane_cols,
):
    rows, width = ev_ref.shape
    event_rows = ev_ref[...].astype(F32)
    normed_o, inv_o = normalize(mixed_ref[...])
    update = up_ref[...].astype(F32)
    gated = (normed_o * update).astype(BF)
    gated_ref[...] = gated
    dp_i, seq_n = lax.axis_index("dp"), lax.axis_size("seq")
    core = lax.rem(dp_i, 2)
    group = (dp_i // 2) * seq_n + lax.axis_index("seq")
    half = plane_cols // 2
    per = width // plane_cols if half else 0
    if not half:
        mine_ref[...] = gated
    for j in range(half):
        g = group ^ j
        base = (g // seq_n) * 2 * seq_n + lax.rem(g, seq_n)
        a0 = pl.multiple_of((base + core * seq_n) * per, per)
        a1 = pl.multiple_of((base + (1 - core) * seq_n) * per, per)
        mine_ref[:, j * per:(j + 1) * per] = gated_ref[:, pl.ds(a0, per)]
        pay_ref[:, j * per:(j + 1) * per] = gated_ref[:, pl.ds(a1, per)]
    layer_out = dot(gated, wo_ref[...]) + event_rows
    inv_norm = lax.rsqrt(jnp.sum(layer_out * layer_out, axis=1, keepdims=True))
    unit = layer_out * inv_norm
    positive = pos_ref[...].astype(F32)
    target = positive * lax.rsqrt(jnp.sum(positive * positive, axis=1, keepdims=True))
    pos_logit = jnp.sum(unit * target, axis=1, keepdims=True) / sharpness_divisor
    neg = jnp.concatenate([neg0_ref[:, :width], neg1_ref[:, :width]], axis=0)
    logs = jnp.concatenate([neg0_ref[:, width:], neg1_ref[:, width:]], axis=0)
    lane = lax.broadcasted_iota(jnp.int32, (rows, logs.shape[1]), 1)
    offset = dot_nt(jnp.where(lane == 0, 1.0, 0.0).astype(BF), logs)
    neg_logit = dot_nt(unit.astype(BF), neg) / sharpness_divisor - offset
    exp_terms = jnp.exp(neg_logit)
    pos_exp = jnp.exp(pos_logit)
    total = pos_exp + jnp.sum(exp_terms, axis=1, keepdims=True)
    weighted = dot(exp_terms.astype(BF), neg)
    grad_unit = (loss_multiplier / sharpness_divisor) * (
        weighted / total + (pos_exp / total - 1.0) * target
    )
    grad_out = (grad_unit - unit * jnp.sum(unit * grad_unit, axis=1, keepdims=True)) * inv_norm
    gout_ref[...] = grad_out
    low = grad_out.astype(BF)
    pay_ref[:, half * per:] = low
    grad_gated = dot_nt(low, wo_ref[...])
    gpu_ref[...] = (grad_gated * normed_o * su_ref[...].astype(F32)).astype(BF)
    gm_ref[...] = norm_back(grad_gated * update, normed_o, inv_o).astype(BF)


def product_kernel(mine_ref, pay_ref, got_ref, own_ref, *send_refs):
    cols = mine_ref.shape[1]
    per = cols // (len(send_refs) + 1)
    low = jnp.concatenate([pay_ref[:, cols:], got_ref[:, cols:]], axis=0)
    gated = jnp.concatenate([mine_ref[...], got_ref[:, :cols]], axis=0)
    out = dot_tn(gated, low)
    own_ref[...] = out[:per]
    for j, send_ref in enumerate(send_refs, 1):
        send_ref[...] = out[j * per:(j + 1) * per].astype(BF)


def sum_kernel(own_ref, *refs):
    *got_refs, kept_ref, give_ref = refs
    mid = kept_ref.shape[0]
    odd = lax.rem(lax.axis_index("pool"), 2) == 1
    total = own_ref[...]
    for got_ref in got_refs:
        total = total + got_ref[...].astype(F32)
    lower, upper = total[:mid], total[mid:]
    kept_ref[...] = jnp.where(odd, upper, lower)
    give_ref[...] = jnp.where(odd, lower, upper).astype(BF)


def join_kernel(kept_ref, got_ref, out_ref):
    mid = kept_ref.shape[0]
    odd = lax.rem(lax.axis_index("pool"), 2) == 1
    kept, got = kept_ref[...].astype(F32), got_ref[...].astype(F32)
    out_ref[:mid] = jnp.where(odd, got, kept)
    out_ref[mid:] = jnp.where(odd, kept, got)


def later_kernel(
    lengths_ref, one_ref, cross_ref, two_ref, far_ref, k_ref, w_ref,
    qn_ref, wn_ref, sn_ref, *, heads, scale,
):
    rows, width = k_ref.shape
    later = wn_ref.shape[0]
    hd = width // heads
    device = lax.axis_index(ALL)
    first_row = device * rows
    l1 = jnp.where(lax.rem(device, 2) == 1, cross_ref[...].astype(F32), one_ref[...].astype(F32))
    l2 = jnp.where(lax.rem(device, 4) < 2, two_ref[...].astype(F32), far_ref[...].astype(F32))
    xn = jnp.concatenate([normalize(e)[0].astype(BF) for e in (l1, l2)], axis=0)
    qn_ref[...] = jax.nn.silu(dot(xn, w_ref[:, width:2 * width])).astype(BF)
    ends = history_ends(lengths_ref, first_row, (8, rows))[0:1]
    row = lax.broadcasted_iota(jnp.int32, (later, rows), 0)
    share = jnp.where(row + (first_row + rows) < ends, 1.0 / EV_DEV, 0.0)
    for h in range(heads):
        c = slice(h * hd, (h + 1) * hd)
        act, slope = silu_and_slope(dot_nt(qn_ref[:, c], k_ref[:, c]) * scale)
        wn_ref[:, c] = (act * share).astype(BF)
        sn_ref[:, c] = (slope * share).astype(BF)


def middle_kernel(
    q_ref, k_ref, v_ref, kh_ref, vh_ref, wt_ref, sl_ref, gm_ref, sq_ref, gpu_ref, w_ref,
    dk_ref, dv_ref, gx_ref, *, heads, scale,
):
    width = q_ref.shape[1]
    early = kh_ref.shape[0]
    hd = width // heads
    grad_q = []
    for h in range(heads):
        c = slice(h * hd, (h + 1) * hd)
        gm = gm_ref[:, c]
        key = jnp.concatenate([kh_ref[:, c], k_ref[:, c]], axis=0)
        val = jnp.concatenate([vh_ref[:, c], v_ref[:, c]], axis=0)
        ds = (dot_nt(gm, val) * sl_ref[h].astype(F32)).astype(BF)
        grad_q.append((dot(ds, key) * scale * sq_ref[:, c].astype(F32)).astype(BF))
        dk_ref[:, c] = dot_tn(ds[:, early:], q_ref[:, c])
        dv_ref[:, c] = dot_tn(wt_ref[h][:, early:], gm)
    gpq = jnp.concatenate(grad_q, axis=1)
    gx_ref[...] = dot_nt(gpu_ref[...], w_ref[:, :width]) + dot_nt(gpq, w_ref[:, width:2 * width])


def last_kernel(
    ev_ref, g1_ref, g2_ref, g2_far_ref, qn_ref, wn_ref, sn_ref, k_ref, v_ref, dk_ref, dv_ref,
    sk_ref, sv_ref, w_ref, gx_ref, gout_ref, out_ref, *, heads, scale,
):
    width = ev_ref.shape[1]
    hd = width // heads
    grad_k, grad_v = [], []
    within = lax.rem(lax.axis_index(ALL), 4) < 2
    for h in range(heads):
        c = slice(h * hd, (h + 1) * hd)
        g2 = jnp.where(within, g2_ref[:, c].astype(F32), g2_far_ref[:, c].astype(F32))
        gm = jnp.concatenate([g1_ref[:, c], g2.astype(BF)], axis=0)
        ds = (dot_nt(gm, v_ref[:, c]) * sn_ref[:, c].astype(F32)).astype(BF)
        gk = (dk_ref[:, c] + dot_tn(ds, qn_ref[:, c])) * scale
        gv = dv_ref[:, c] + dot_tn(wn_ref[:, c], gm)
        grad_k.append((gk * sk_ref[:, c].astype(F32)).astype(BF))
        grad_v.append((gv * sv_ref[:, c].astype(F32)).astype(BF))
    grad_x = (
        gx_ref[...]
        + dot_nt(jnp.concatenate(grad_k, axis=1), w_ref[:, 2 * width:3 * width])
        + dot_nt(jnp.concatenate(grad_v, axis=1), w_ref[:, 3 * width:])
    )
    normed_x, inv_x = normalize(ev_ref[...].astype(F32))
    out_ref[...] = norm_back(grad_x, normed_x, inv_x) + gout_ref[...]


def call(kernel, outs, flops, *args, scalars=False, scratch=(), far=()):
    vmem = pl.BlockSpec(memory_space=pltpu.VMEM)
    specs = [vmem] * len(args)
    if scalars:
        specs[0] = pl.BlockSpec(memory_space=pltpu.SMEM)
    for i in far:
        specs[i] = pl.BlockSpec(memory_space=pltpu.HBM)
    return pl.pallas_call(
        kernel,
        in_specs=specs,
        out_specs=[vmem] * len(outs),
        out_shape=list(outs),
        scratch_shapes=list(scratch),
        cost_estimate=cost(flops, *args, *outs),
        compiler_params=pltpu.CompilerParams(vmem_limit_bytes=VMEM_BYTES),
    )(*args)


def shaped(shape, dtype):
    return jax.ShapeDtypeStruct(shape, dtype)


def cost(flops, *arrays):
    return pl.CostEstimate(
        flops=flops,
        bytes_accessed=sum(math.prod(x.shape) * x.dtype.itemsize for x in arrays),
        transcendentals=0,
    )


def layer(events, input_weight, output_weight, positives, negatives, log_probs, lengths):
    rows, width = events.shape
    hd = width // HEADS
    scale = 1.0 / math.sqrt(hd)
    early = REACH * rows
    keys = early + rows
    low_block = shaped((rows, width), BF)
    wide_block = shaped((rows, width), F32)

    dp_n, seq_n = lax.axis_size("dp"), lax.axis_size("seq")
    plane_n = dp_n * seq_n
    half = plane_n // 2
    paired = width % (plane_n * 128) == 0 and is_pow2(half) and half > 0
    sent = width // 2 if paired else 0

    near = neighbours(events)
    part = negatives.shape[0] // plane_n
    if part % 16 == 0:
        piece, = call(
            piece_kernel, [shaped((part, width + 128), BF)], 0,
            negatives, log_probs[None, :],
        )
    else:
        at = lax.axis_index(PLANE) * part
        raw = lax.dynamic_slice_in_dim(negatives, at, part, 0).astype(F32)
        unit = raw * lax.rsqrt(jnp.sum(raw * raw, axis=1, keepdims=True))
        logs = lax.dynamic_slice_in_dim(log_probs, at, part, 0)
        piece = jnp.concatenate(
            [unit.astype(BF), jnp.broadcast_to(logs[:, None], (part, 128))], axis=1
        )
    neg0, neg1 = gathered(piece)

    flops = 2 * rows * width * width
    up, q, k, v, s_up, s_q, s_k, s_v = call(
        own_kernel, [low_block] * 8, 4 * flops, events, input_weight
    )
    weight = input_weight

    early_block = shaped((early, width), BF)
    head_block = shaped((HEADS, rows, keys), BF)
    kh, vh, wts, slopes, mixed = call(
        functools.partial(attend_kernel, heads=HEADS, scale=scale),
        [early_block, early_block, head_block, head_block, wide_block], 5 * flops,
        lengths, *near, q, k, v, weight, scalars=True,
    )
    mine, pay, grad_out, gpu, gm = call(
        functools.partial(loss_kernel, plane_cols=plane_n if paired else 0),
        [
            shaped((rows, sent or width), BF), shaped((rows, sent + width), BF),
            wide_block, low_block, low_block,
        ],
        4 * flops, mixed, events, positives, neg0, neg1, s_up, up, output_weight,
        scratch=[pltpu.VMEM((rows, width), BF)],
    )

    if paired:
        got = swapped(pay, "dp", 1)
        own_sum, *sends = call(
            product_kernel,
            [shaped((width // plane_n, width), F32)]
            + [shaped((width // plane_n, width), BF)] * (half - 1),
            flops, mine, pay, got,
        )
        terms = [own_sum]
        for j in range(1, half):
            pairs = []
            for i in range(plane_n):
                d, s = divmod(i, seq_n)
                t = ((d // 2) * seq_n + s) ^ j
                pairs.append((i, ((t // seq_n) * 2 + d % 2) * seq_n + t % seq_n))
            terms.append(lax.ppermute(sends[j - 1], PLANE, pairs))
    else:
        terms = [lax.psum_scatter(dot_tn(mine, pay), PLANE, scatter_dimension=0, tiled=True)]

    g2, g2_far = two_later(gm)
    g1 = shifted(gm, -1)

    qn, wn, sn = call(
        functools.partial(later_kernel, heads=HEADS, scale=scale),
        [early_block] * 3, 3 * flops, lengths, *near, k, weight, scalars=True,
    )
    dk, dv, gx = call(
        functools.partial(middle_kernel, heads=HEADS, scale=scale),
        [wide_block] * 3, 4 * flops,
        q, k, v, kh, vh, wts, slopes, gm, s_q, gpu, weight,
    )

    pool_n = lax.axis_size("pool")
    if is_pow2(pool_n) and pool_n > 2:
        rows_out = terms[0].shape[0]
        kept, give = call(
            sum_kernel,
            [shaped((rows_out // 2, width), F32), shaped((rows_out // 2, width), BF)], 0, *terms,
        )
        kept = kept + swapped(give, "pool", 1).astype(F32)
        for b in range(1, pool_n.bit_length() - 1):
            low = kept.astype(BF)
            kept = low.astype(F32) + swapped(low, "pool", 1 << b).astype(F32)
        low = kept.astype(BF)
        other = swapped(low, "pool", 1)
        total, = call(join_kernel, [shaped((rows_out, width), F32)], 0, low, other)
    else:
        total = lax.psum(sum(t.astype(F32) for t in terms), "pool")

    d_events, = call(
        functools.partial(last_kernel, heads=HEADS, scale=scale),
        [wide_block], 4 * flops,
        events, g1, g2, g2_far, qn, wn, sn, k, v, dk, dv, s_k, s_v, weight, gx, grad_out,
    )
    return (d_events, total)


def solution(mesh):
    placed = (
        P(("dp", "seq", "pool"), None),
        P(),
        P(),
        P(("dp", "seq", "pool"), None),
        P("pool", None),
        P("pool"),
        P(),
    )
    return jax.shard_map(
        layer,
        mesh=mesh,
        in_specs=placed,
        out_specs=(P(("dp", "seq", "pool"), None), P(("dp", "seq"), None)),
        check_vma=False,
    )
```

```python
import functools
import math

import jax
import jax.numpy as jnp
from jax import lax
from jax.experimental import pallas as pl
from jax.experimental.pallas import tpu as pltpu
from jax.sharding import PartitionSpec as P


HEADS = 8
EV_DEV = 128
REACH = 2

epsilon = 1e-05
sharpness_divisor = 0.05
loss_multiplier = 8.0

ALL = ("dp", "seq", "pool")
PLANE = ("dp", "seq")
VMEM_BYTES = 16 << 20
BF = jnp.bfloat16
F32 = jnp.float32

NT = (((1,), (1,)), ((), ()))
TN = (((0,), (0,)), ((), ()))


def dot(a, b):
    return jnp.dot(a, b, preferred_element_type=F32)


def dot_nt(a, b):
    return lax.dot_general(a, b, NT, preferred_element_type=F32)


def dot_tn(a, b):
    return lax.dot_general(a, b, TN, preferred_element_type=F32)


def shifted(x, by):
    length = lax.axis_size(ALL)
    pairs = [(i, i + by) for i in range(length) if 0 <= i + by < length]
    return lax.ppermute(x, ALL, pairs)


def neighbours(x):
    n = lax.axis_size(ALL)
    two = lax.ppermute(x, ALL, [(i, i ^ 2) for i in range(n)])
    odd = [(i, i + 1) for i in range(1, n - 1, 2)]
    cross = lax.ppermute(x, ALL, odd + [(j, i) for i, j in odd])
    one = lax.ppermute(x, ALL, [(i, i ^ 1) for i in range(n)])
    if lax.axis_size("pool") == 4:
        source, by = two, 4
    else:
        source, by = x, -2
    pairs = [(i, i + by if i % 4 < 2 else i - by) for i in range(n)]
    far = lax.ppermute(source, ALL, [(i, j) for i, j in pairs if 0 <= j < n])
    return one, cross, two, far


def later_blocks(x):
    n = lax.axis_size(ALL)
    if lax.axis_size("pool") != 4:
        one, two = shifted(x, -1), shifted(x, -2)
        return one, one, two, two
    two = lax.ppermute(x, ALL, [(i, i ^ 2) for i in range(n)])
    one = lax.ppermute(x, ALL, [(i, i ^ 1) for i in range(n)])
    far = lax.ppermute(two, ALL, [(i, i - 4) for i in range(4, n) if i % 4 >= 2])
    next_one = [(i, i + 1) for i in range(0, n, 4)] + [(i, i - 3) for i in range(6, n, 4)]
    return one, lax.ppermute(two, ALL, next_one), two, far


def is_pow2(n):
    return n & (n - 1) == 0


def swapped(x, axis, bit):
    return lax.ppermute(x, axis, [(i, i ^ bit) for i in range(lax.axis_size(axis))])


def gather_stages(sizes):
    stages = []
    for axis in PLANE[::-1]:
        stages += [(axis, 1 << b) for b in reversed(range(sizes[axis].bit_length() - 1))]
    return stages


def gathered(x):
    sizes = {axis: lax.axis_size(axis) for axis in ALL}
    if all(is_pow2(n) for n in sizes.values()):
        parts = [x] + [swapped(x, "pool", k) for k in range(1, sizes["pool"])]
        for axis, bit in gather_stages(sizes):
            x = jnp.concatenate(parts, axis=0)
            parts = [x, swapped(x, axis, bit)]
        return parts
    for axis, n in sizes.items():
        turns = [lax.ppermute(x, axis, [(i, (i + k) % n) for i in range(n)]) for k in range(1, n)]
        x = jnp.concatenate([x] + turns, axis=0)
    return [x[:x.shape[0] // 2], x[x.shape[0] // 2:]]


def normalize(row_data):
    centred = row_data - jnp.mean(row_data, axis=1, keepdims=True)
    inv_std = lax.rsqrt(jnp.mean(centred * centred, axis=1, keepdims=True) + epsilon)
    return centred * inv_std, inv_std


def norm_back(grad_in, normed, inv_std):
    return (
        grad_in
        - jnp.mean(grad_in, axis=1, keepdims=True)
        - normed * jnp.mean(grad_in * normed, axis=1, keepdims=True)
    ) * inv_std


def silu_and_slope(v):
    sig = jax.nn.sigmoid(v)
    return v * sig, sig * (1.0 + v * (1.0 - sig))


def own_kernel(x_ref, w_ref, *out_refs):
    width = x_ref.shape[1]
    parts = len(out_refs) // 2
    xn = normalize(x_ref[...].astype(F32))[0].astype(BF)
    for i in range(parts):
        act, slope = silu_and_slope(dot(xn, w_ref[:, i * width:(i + 1) * width]))
        out_refs[i][...] = act.astype(BF)
        out_refs[parts + i][...] = slope.astype(BF)


def history_ends(lengths_ref, first, shape):
    column = first + lax.broadcasted_iota(jnp.int32, shape, 1)
    far = jnp.full(shape, jnp.iinfo(jnp.int32).max, jnp.int32)

    def body(u, carry):
        end, found = carry
        end = end + lengths_ref[u]
        return end, jnp.minimum(found, jnp.where(end > column, end, far))

    found = lax.fori_loop(0, lengths_ref.shape[0], body, (jnp.int32(0), far))[1]
    return jnp.where(column >= 0, found, 0)


def piece_kernel(neg_ref, log_ref, out_ref):
    part = out_ref.shape[0]
    width = neg_ref.shape[1]
    at = pl.multiple_of(lax.axis_index(PLANE) * part, part)
    raw = neg_ref[pl.ds(at, part), :].astype(F32)
    out_ref[:, :width] = (
        raw * lax.rsqrt(jnp.sum(raw * raw, axis=1, keepdims=True))
    ).astype(BF)
    logs = log_ref[...].astype(F32)
    shape = (part, logs.shape[1])
    wanted = lax.broadcasted_iota(jnp.int32, shape, 1) == at + lax.broadcasted_iota(
        jnp.int32, shape, 0
    )
    mine = jnp.sum(jnp.where(wanted, logs, 0.0), axis=1, keepdims=True)
    out_ref[:, width:] = jnp.broadcast_to(mine, (part, 128)).astype(BF)


def attend_kernel(
    lengths_ref, one_ref, cross_ref, two_ref, far_ref, q_ref, k_ref, v_ref, w_ref,
    kh_ref, vh_ref, wt_ref, sl_ref, mixed_ref, *, heads, scale,
):
    rows, width = q_ref.shape
    early = kh_ref.shape[0]
    keys = early + rows
    hd = width // heads
    device = lax.axis_index(ALL)
    first_row = device * rows
    e2 = jnp.where(lax.rem(device, 4) < 2, far_ref[...].astype(F32), two_ref[...].astype(F32))
    e1 = jnp.where(lax.rem(device, 2) == 1, one_ref[...].astype(F32), cross_ref[...].astype(F32))
    xn = jnp.concatenate([normalize(e)[0].astype(BF) for e in (e2, e1)], axis=0)
    kh_ref[...] = jax.nn.silu(dot(xn, w_ref[:, 2 * width:3 * width])).astype(BF)
    vh_ref[...] = jax.nn.silu(dot(xn, w_ref[:, 3 * width:])).astype(BF)
    ends = history_ends(lengths_ref, first_row - early, (8, keys))[0:1]
    col = lax.broadcasted_iota(jnp.int32, (rows, keys), 1)
    row = lax.broadcasted_iota(jnp.int32, (rows, keys), 0)
    allowed = (row + first_row < ends) & (col <= row + early)
    share = jnp.where(allowed, 1.0 / EV_DEV, 0.0)
    for h in range(heads):
        c = slice(h * hd, (h + 1) * hd)
        key = jnp.concatenate([kh_ref[:, c], k_ref[:, c]], axis=0)
        val = jnp.concatenate([vh_ref[:, c], v_ref[:, c]], axis=0)
        act, slope = silu_and_slope(dot_nt(q_ref[:, c], key) * scale)
        wts = (act * share).astype(BF)
        wt_ref[h] = wts
        sl_ref[h] = (slope * share).astype(BF)
        mixed_ref[:, c] = dot(wts, val)


def output_kernel(
    mixed_ref, ev_ref, pos_ref, up_ref, wo_ref,
    mine_ref, give_ref, normed_ref, inv_ref, unit_ref, target_ref, gated_ref, *, plane_cols,
):
    width = ev_ref.shape[1]
    normed_o, inv_o = normalize(mixed_ref[...])
    gated = (normed_o * up_ref[...].astype(F32)).astype(BF)
    normed_ref[...] = normed_o
    gated_ref[...] = gated
    dp_i, seq_n = lax.axis_index("dp"), lax.axis_size("seq")
    core = lax.rem(dp_i, 2)
    group = (dp_i // 2) * seq_n + lax.axis_index("seq")
    half = plane_cols // 2
    per = width // plane_cols if half else 0
    if not half:
        mine_ref[...] = gated
        give_ref[...] = gated[:, :give_ref.shape[1]]
    for j in range(half):
        g = group ^ j
        base = (g // seq_n) * 2 * seq_n + lax.rem(g, seq_n)
        a0 = pl.multiple_of((base + core * seq_n) * per, per)
        a1 = pl.multiple_of((base + (1 - core) * seq_n) * per, per)
        mine_ref[:, j * per:(j + 1) * per] = gated_ref[:, pl.ds(a0, per)]
        give_ref[:, j * per:(j + 1) * per] = gated_ref[:, pl.ds(a1, per)]
    layer_out = dot(gated, wo_ref[...]) + ev_ref[...].astype(F32)
    inv_norm = lax.rsqrt(jnp.sum(layer_out * layer_out, axis=1, keepdims=True))
    unit = layer_out * inv_norm
    positive = pos_ref[...].astype(F32)
    target = positive * lax.rsqrt(jnp.sum(positive * positive, axis=1, keepdims=True))
    pos_logit = jnp.sum(unit * target, axis=1, keepdims=True) / sharpness_divisor
    unit_ref[...] = unit
    target_ref[...] = target
    inv_ref[...] = jnp.concatenate([inv_o, inv_norm, pos_logit], axis=1)


def loss_kernel(
    unit_ref, target_ref, inv_ref, neg0_ref, neg1_ref, give_ref, pay_ref, gout_ref, low_ref,
):
    rows, width = unit_ref.shape
    unit, target = unit_ref[...], target_ref[...]
    inv_norm, pos_logit = inv_ref[:, 1:2], inv_ref[:, 2:3]
    neg = jnp.concatenate([neg0_ref[:, :width], neg1_ref[:, :width]], axis=0)
    logs = jnp.concatenate([neg0_ref[:, width:], neg1_ref[:, width:]], axis=0)
    lane = lax.broadcasted_iota(jnp.int32, (rows, logs.shape[1]), 1)
    offset = dot_nt(jnp.where(lane == 0, 1.0, 0.0).astype(BF), logs)
    neg_logit = dot_nt(unit.astype(BF), neg) / sharpness_divisor - offset
    exp_terms = jnp.exp(neg_logit)
    pos_exp = jnp.exp(pos_logit)
    total = pos_exp + jnp.sum(exp_terms, axis=1, keepdims=True)
    weighted = dot(exp_terms.astype(BF), neg)
    grad_unit = (loss_multiplier / sharpness_divisor) * (
        weighted / total + (pos_exp / total - 1.0) * target
    )
    grad_out = (grad_unit - unit * jnp.sum(unit * grad_unit, axis=1, keepdims=True)) * inv_norm
    gout_ref[...] = grad_out
    low = grad_out.astype(BF)
    low_ref[...] = low
    sent = pay_ref.shape[1] - width
    if sent:
        pay_ref[:, :sent] = give_ref[...]
    pay_ref[:, sent:] = low


def back_kernel(low_ref, normed_ref, inv_ref, su_ref, up_ref, wo_ref, gpu_ref, gm_ref):
    normed_o = normed_ref[...]
    grad_gated = dot_nt(low_ref[...], wo_ref[...])
    gpu_ref[...] = (grad_gated * normed_o * su_ref[...].astype(F32)).astype(BF)
    gm_ref[...] = norm_back(
        grad_gated * up_ref[...].astype(F32), normed_o, inv_ref[:, 0:1]
    ).astype(BF)


def product_kernel(mine_ref, pay_ref, got_ref, own_ref, *send_refs):
    cols = mine_ref.shape[1]
    per = cols // (len(send_refs) + 1)
    low = jnp.concatenate([pay_ref[:, cols:], got_ref[:, cols:]], axis=0)
    gated = jnp.concatenate([mine_ref[...], got_ref[:, :cols]], axis=0)
    out = dot_tn(gated, low)
    own_ref[...] = out[:per]
    for j, send_ref in enumerate(send_refs, 1):
        send_ref[...] = out[j * per:(j + 1) * per].astype(BF)


def sum_kernel(own_ref, *refs):
    *got_refs, kept_ref, give_ref = refs
    mid = kept_ref.shape[0]
    odd = lax.rem(lax.axis_index("pool"), 2) == 1
    total = own_ref[...]
    for got_ref in got_refs:
        total = total + got_ref[...].astype(F32)
    lower, upper = total[:mid], total[mid:]
    kept_ref[...] = jnp.where(odd, upper, lower)
    give_ref[...] = jnp.where(odd, lower, upper).astype(BF)


def join_kernel(kept_ref, got_ref, out_ref):
    mid = kept_ref.shape[0]
    odd = lax.rem(lax.axis_index("pool"), 2) == 1
    kept, got = kept_ref[...].astype(F32), got_ref[...].astype(F32)
    out_ref[:mid] = jnp.where(odd, got, kept)
    out_ref[mid:] = jnp.where(odd, kept, got)


def later_kernel(
    lengths_ref, one_ref, cross_ref, two_ref, far_ref, k_ref, w_ref,
    qn_ref, wn_ref, sn_ref, *, heads, scale,
):
    rows, width = k_ref.shape
    later = wn_ref.shape[0]
    hd = width // heads
    device = lax.axis_index(ALL)
    first_row = device * rows
    l1 = jnp.where(lax.rem(device, 2) == 1, cross_ref[...].astype(F32), one_ref[...].astype(F32))
    l2 = jnp.where(lax.rem(device, 4) < 2, two_ref[...].astype(F32), far_ref[...].astype(F32))
    xn = jnp.concatenate([normalize(e)[0].astype(BF) for e in (l1, l2)], axis=0)
    qn_ref[...] = jax.nn.silu(dot(xn, w_ref[:, width:2 * width])).astype(BF)
    ends = history_ends(lengths_ref, first_row, (8, rows))[0:1]
    row = lax.broadcasted_iota(jnp.int32, (later, rows), 0)
    share = jnp.where(row + (first_row + rows) < ends, 1.0 / EV_DEV, 0.0)
    for h in range(heads):
        c = slice(h * hd, (h + 1) * hd)
        act, slope = silu_and_slope(dot_nt(qn_ref[:, c], k_ref[:, c]) * scale)
        wn_ref[:, c] = (act * share).astype(BF)
        sn_ref[:, c] = (slope * share).astype(BF)


def middle_kernel(
    q_ref, k_ref, v_ref, kh_ref, vh_ref, wt_ref, sl_ref, gm_ref, sq_ref, gpu_ref, w_ref,
    dk_ref, dv_ref, gx_ref, *, heads, scale,
):
    width = q_ref.shape[1]
    early = kh_ref.shape[0]
    hd = width // heads
    grad_q = []
    for h in range(heads):
        c = slice(h * hd, (h + 1) * hd)
        gm = gm_ref[:, c]
        key = jnp.concatenate([kh_ref[:, c], k_ref[:, c]], axis=0)
        val = jnp.concatenate([vh_ref[:, c], v_ref[:, c]], axis=0)
        ds = (dot_nt(gm, val) * sl_ref[h].astype(F32)).astype(BF)
        grad_q.append((dot(ds, key) * scale * sq_ref[:, c].astype(F32)).astype(BF))
        dk_ref[:, c] = dot_tn(ds[:, early:], q_ref[:, c])
        dv_ref[:, c] = dot_tn(wt_ref[h][:, early:], gm)
    gpq = jnp.concatenate(grad_q, axis=1)
    gx_ref[...] = dot_nt(gpu_ref[...], w_ref[:, :width]) + dot_nt(gpq, w_ref[:, width:2 * width])


def last_kernel(
    ev_ref, g1_ref, g1_odd_ref, g2_ref, g2_far_ref, qn_ref, wn_ref, sn_ref, k_ref, v_ref, dk_ref, dv_ref,
    sk_ref, sv_ref, w_ref, gx_ref, gout_ref, out_ref, *, heads, scale,
):
    width = ev_ref.shape[1]
    hd = width // heads
    grad_k, grad_v = [], []
    device = lax.axis_index(ALL)
    odd, within = lax.rem(device, 2) == 1, lax.rem(device, 4) < 2
    for h in range(heads):
        c = slice(h * hd, (h + 1) * hd)
        g2 = jnp.where(within, g2_ref[:, c].astype(F32), g2_far_ref[:, c].astype(F32))
        g1 = jnp.where(odd, g1_odd_ref[:, c].astype(F32), g1_ref[:, c].astype(F32))
        gm = jnp.concatenate([g1, g2], axis=0).astype(BF)
        ds = (dot_nt(gm, v_ref[:, c]) * sn_ref[:, c].astype(F32)).astype(BF)
        gk = (dk_ref[:, c] + dot_tn(ds, qn_ref[:, c])) * scale
        gv = dv_ref[:, c] + dot_tn(wn_ref[:, c], gm)
        grad_k.append((gk * sk_ref[:, c].astype(F32)).astype(BF))
        grad_v.append((gv * sv_ref[:, c].astype(F32)).astype(BF))
    grad_x = (
        gx_ref[...]
        + dot_nt(jnp.concatenate(grad_k, axis=1), w_ref[:, 2 * width:3 * width])
        + dot_nt(jnp.concatenate(grad_v, axis=1), w_ref[:, 3 * width:])
    )
    normed_x, inv_x = normalize(ev_ref[...].astype(F32))
    out_ref[...] = norm_back(grad_x, normed_x, inv_x) + gout_ref[...]


def call(kernel, outs, flops, *args, scalars=False, scratch=(), far=()):
    vmem = pl.BlockSpec(memory_space=pltpu.VMEM)
    specs = [vmem] * len(args)
    if scalars:
        specs[0] = pl.BlockSpec(memory_space=pltpu.SMEM)
    for i in far:
        specs[i] = pl.BlockSpec(memory_space=pltpu.HBM)
    return pl.pallas_call(
        kernel,
        in_specs=specs,
        out_specs=[vmem] * len(outs),
        out_shape=list(outs),
        scratch_shapes=list(scratch),
        cost_estimate=cost(flops, *args, *outs),
        compiler_params=pltpu.CompilerParams(vmem_limit_bytes=VMEM_BYTES),
    )(*args)


def shaped(shape, dtype):
    return jax.ShapeDtypeStruct(shape, dtype)


def cost(flops, *arrays):
    return pl.CostEstimate(
        flops=flops,
        bytes_accessed=sum(math.prod(x.shape) * x.dtype.itemsize for x in arrays),
        transcendentals=0,
    )


def layer(events, input_weight, output_weight, positives, negatives, log_probs, lengths):
    rows, width = events.shape
    hd = width // HEADS
    scale = 1.0 / math.sqrt(hd)
    early = REACH * rows
    keys = early + rows
    low_block = shaped((rows, width), BF)
    wide_block = shaped((rows, width), F32)

    dp_n, seq_n = lax.axis_size("dp"), lax.axis_size("seq")
    plane_n = dp_n * seq_n
    half = plane_n // 2
    paired = width % (plane_n * 128) == 0 and is_pow2(half) and half > 0
    sent = width // 2 if paired else 0

    near = neighbours(events)
    part = negatives.shape[0] // plane_n
    if part % 16 == 0:
        piece, = call(
            piece_kernel, [shaped((part, width + 128), BF)], 0,
            negatives, log_probs[None, :],
        )
    else:
        at = lax.axis_index(PLANE) * part
        raw = lax.dynamic_slice_in_dim(negatives, at, part, 0).astype(F32)
        unit = raw * lax.rsqrt(jnp.sum(raw * raw, axis=1, keepdims=True))
        logs = lax.dynamic_slice_in_dim(log_probs, at, part, 0)
        piece = jnp.concatenate(
            [unit.astype(BF), jnp.broadcast_to(logs[:, None], (part, 128))], axis=1
        )
    neg0, neg1 = gathered(piece)

    flops = 2 * rows * width * width
    up, q, k, v, s_up, s_q, s_k, s_v = call(
        own_kernel, [low_block] * 8, 4 * flops, events, input_weight
    )
    weight = input_weight

    early_block = shaped((early, width), BF)
    head_block = shaped((HEADS, rows, keys), BF)
    kh, vh, wts, slopes, mixed = call(
        functools.partial(attend_kernel, heads=HEADS, scale=scale),
        [early_block, early_block, head_block, head_block, wide_block], 5 * flops,
        lengths, *near, q, k, v, weight, scalars=True,
    )
    mine, give, normed_o, inverses, unit, target = call(
        functools.partial(output_kernel, plane_cols=plane_n if paired else 0),
        [
            shaped((rows, sent or width), BF), shaped((rows, sent or 128), BF),
            wide_block, shaped((rows, 3), F32), wide_block, wide_block,
        ],
        flops, mixed, events, positives, up, output_weight,
        scratch=[pltpu.VMEM((rows, width), BF)],
    )
    pay, grad_out, low = call(
        loss_kernel,
        [shaped((rows, sent + width), BF), wide_block, low_block],
        2 * flops, unit, target, inverses, neg0, neg1, give,
    )
    gpu, gm = call(
        back_kernel, [low_block, low_block],
        flops, low, normed_o, inverses, s_up, up, output_weight,
    )

    if paired:
        got = swapped(pay, "dp", 1)
        own_sum, *sends = call(
            product_kernel,
            [shaped((width // plane_n, width), F32)]
            + [shaped((width // plane_n, width), BF)] * (half - 1),
            flops, mine, pay, got,
        )
        terms = [own_sum]
        for j in range(1, half):
            pairs = []
            for i in range(plane_n):
                d, s = divmod(i, seq_n)
                t = ((d // 2) * seq_n + s) ^ j
                pairs.append((i, ((t // seq_n) * 2 + d % 2) * seq_n + t % seq_n))
            terms.append(lax.ppermute(sends[j - 1], PLANE, pairs))
    else:
        terms = [lax.psum_scatter(dot_tn(mine, pay), PLANE, scatter_dimension=0, tiled=True)]

    later = later_blocks(gm)

    qn, wn, sn = call(
        functools.partial(later_kernel, heads=HEADS, scale=scale),
        [early_block] * 3, 3 * flops, lengths, *near, k, weight, scalars=True,
    )
    dk, dv, gx = call(
        functools.partial(middle_kernel, heads=HEADS, scale=scale),
        [wide_block] * 3, 4 * flops,
        q, k, v, kh, vh, wts, slopes, gm, s_q, gpu, weight,
    )

    pool_n = lax.axis_size("pool")
    if is_pow2(pool_n) and pool_n > 2:
        rows_out = terms[0].shape[0]
        kept, give = call(
            sum_kernel,
            [shaped((rows_out // 2, width), F32), shaped((rows_out // 2, width), BF)], 0, *terms,
        )
        kept = kept + swapped(give, "pool", 1).astype(F32)
        for b in range(1, pool_n.bit_length() - 1):
            low = kept.astype(BF)
            kept = low.astype(F32) + swapped(low, "pool", 1 << b).astype(F32)
        low = kept.astype(BF)
        other = swapped(low, "pool", 1)
        total, = call(join_kernel, [shaped((rows_out, width), F32)], 0, low, other)
    else:
        total = lax.psum(sum(t.astype(F32) for t in terms), "pool")

    d_events, = call(
        functools.partial(last_kernel, heads=HEADS, scale=scale),
        [wide_block], 4 * flops,
        events, *later, qn, wn, sn, k, v, dk, dv, s_k, s_v, weight, gx, grad_out,
    )
    return (d_events, total)


def solution(mesh):
    placed = (
        P(("dp", "seq", "pool"), None),
        P(),
        P(),
        P(("dp", "seq", "pool"), None),
        P("pool", None),
        P("pool"),
        P(),
    )
    return jax.shard_map(
        layer,
        mesh=mesh,
        in_specs=placed,
        out_specs=(P(("dp", "seq", "pool"), None), P(("dp", "seq"), None)),
        check_vma=False,
    )
```

```python
import functools
import math

import jax
import jax.numpy as jnp
from jax import lax
from jax.experimental import pallas as pl
from jax.experimental.pallas import tpu as pltpu
from jax.sharding import PartitionSpec as P


HEADS = 8
EV_DEV = 128
REACH = 2

epsilon = 1e-05
sharpness_divisor = 0.05
loss_multiplier = 8.0

ALL = ("dp", "seq", "pool")
PLANE = ("dp", "seq")
VMEM_BYTES = 16 << 20
BF = jnp.bfloat16
F32 = jnp.float32

NT = (((1,), (1,)), ((), ()))
TN = (((0,), (0,)), ((), ()))


def dot(a, b):
    return jnp.dot(a, b, preferred_element_type=F32)


def dot_nt(a, b):
    return lax.dot_general(a, b, NT, preferred_element_type=F32)


def dot_tn(a, b):
    return lax.dot_general(a, b, TN, preferred_element_type=F32)


def shifted(x, by):
    length = lax.axis_size(ALL)
    pairs = [(i, i + by) for i in range(length) if 0 <= i + by < length]
    return lax.ppermute(x, ALL, pairs)


def neighbours(x):
    n = lax.axis_size(ALL)
    two = lax.ppermute(x, ALL, [(i, i ^ 2) for i in range(n)])
    odd = [(i, i + 1) for i in range(1, n - 1, 2)]
    cross = lax.ppermute(x, ALL, odd + [(j, i) for i, j in odd])
    one = lax.ppermute(x, ALL, [(i, i ^ 1) for i in range(n)])
    if lax.axis_size("pool") == 4:
        source, by = two, 4
    else:
        source, by = x, -2
    pairs = [(i, i + by if i % 4 < 2 else i - by) for i in range(n)]
    far = lax.ppermute(source, ALL, [(i, j) for i, j in pairs if 0 <= j < n])
    return one, cross, two, far


def later_blocks(x):
    n = lax.axis_size(ALL)
    if lax.axis_size("pool") != 4:
        one, two = shifted(x, -1), shifted(x, -2)
        return one, one, two, two
    two = lax.ppermute(x, ALL, [(i, i ^ 2) for i in range(n)])
    one = lax.ppermute(x, ALL, [(i, i ^ 1) for i in range(n)])
    far = lax.ppermute(two, ALL, [(i, i - 4) for i in range(4, n) if i % 4 >= 2])
    next_one = [(i, i + 1) for i in range(0, n, 4)] + [(i, i - 3) for i in range(6, n, 4)]
    return one, lax.ppermute(two, ALL, next_one), two, far


def is_pow2(n):
    return n & (n - 1) == 0


def swapped(x, axis, bit):
    return lax.ppermute(x, axis, [(i, i ^ bit) for i in range(lax.axis_size(axis))])


def gather_stages(sizes):
    stages = []
    for axis in PLANE[::-1]:
        stages += [(axis, 1 << b) for b in reversed(range(sizes[axis].bit_length() - 1))]
    return stages


def gathered(x):
    sizes = {axis: lax.axis_size(axis) for axis in ALL}
    if all(is_pow2(n) for n in sizes.values()):
        parts = [x] + [swapped(x, "pool", k) for k in range(1, sizes["pool"])]
        for axis, bit in gather_stages(sizes):
            x = jnp.concatenate(parts, axis=0)
            parts = [x, swapped(x, axis, bit)]
        return parts
    for axis, n in sizes.items():
        turns = [lax.ppermute(x, axis, [(i, (i + k) % n) for i in range(n)]) for k in range(1, n)]
        x = jnp.concatenate([x] + turns, axis=0)
    return [x[:x.shape[0] // 2], x[x.shape[0] // 2:]]


def normalize(row_data):
    centred = row_data - jnp.mean(row_data, axis=1, keepdims=True)
    inv_std = lax.rsqrt(jnp.mean(centred * centred, axis=1, keepdims=True) + epsilon)
    return centred * inv_std, inv_std


def norm_back(grad_in, normed, inv_std):
    return (
        grad_in
        - jnp.mean(grad_in, axis=1, keepdims=True)
        - normed * jnp.mean(grad_in * normed, axis=1, keepdims=True)
    ) * inv_std


def silu_and_slope(v):
    sig = jax.nn.sigmoid(v)
    return v * sig, sig * (1.0 + v * (1.0 - sig))


def own_kernel(x_ref, w_ref, copy_ref, *out_refs):
    width = x_ref.shape[1]
    parts = len(out_refs) // 2
    copy_ref[...] = x_ref[...]
    xn = normalize(x_ref[...].astype(F32))[0].astype(BF)
    for i in range(parts):
        act, slope = silu_and_slope(dot(xn, w_ref[:, i * width:(i + 1) * width]))
        out_refs[i][...] = act.astype(BF)
        out_refs[parts + i][...] = slope.astype(BF)


def history_ends(lengths_ref, first, shape):
    column = first + lax.broadcasted_iota(jnp.int32, shape, 1)
    far = jnp.full(shape, jnp.iinfo(jnp.int32).max, jnp.int32)

    def body(u, carry):
        end, found = carry
        end = end + lengths_ref[u]
        return end, jnp.minimum(found, jnp.where(end > column, end, far))

    found = lax.fori_loop(0, lengths_ref.shape[0], body, (jnp.int32(0), far))[1]
    return jnp.where(column >= 0, found, 0)


def piece_kernel(neg_ref, log_ref, out_ref):
    part = out_ref.shape[0]
    width = neg_ref.shape[1]
    at = pl.multiple_of(lax.axis_index(PLANE) * part, part)
    raw = neg_ref[pl.ds(at, part), :].astype(F32)
    out_ref[:, :width] = (
        raw * lax.rsqrt(jnp.sum(raw * raw, axis=1, keepdims=True))
    ).astype(BF)
    logs = log_ref[...].astype(F32)
    shape = (part, logs.shape[1])
    wanted = lax.broadcasted_iota(jnp.int32, shape, 1) == at + lax.broadcasted_iota(
        jnp.int32, shape, 0
    )
    mine = jnp.sum(jnp.where(wanted, logs, 0.0), axis=1, keepdims=True)
    out_ref[:, width:] = jnp.broadcast_to(mine, (part, 128)).astype(BF)


def self_kernel(lengths_ref, q_ref, k_ref, v_ref, wt_ref, sl_ref, mixed_ref, *, heads, scale):
    rows, width = q_ref.shape
    hd = width // heads
    first_row = lax.axis_index(ALL) * rows
    ends = history_ends(lengths_ref, first_row, (8, rows))[0:1]
    col = lax.broadcasted_iota(jnp.int32, (rows, rows), 1)
    row = lax.broadcasted_iota(jnp.int32, (rows, rows), 0)
    share = jnp.where((row + first_row < ends) & (col <= row), 1.0 / EV_DEV, 0.0)
    for h in range(heads):
        c = slice(h * hd, (h + 1) * hd)
        act, slope = silu_and_slope(dot_nt(q_ref[:, c], k_ref[:, c]) * scale)
        wts = (act * share).astype(BF)
        wt_ref[h] = wts
        sl_ref[h] = (slope * share).astype(BF)
        mixed_ref[:, c] = dot(wts, v_ref[:, c])


def attend_kernel(
    lengths_ref, one_ref, cross_ref, two_ref, far_ref, q_ref, self_ref, w_ref,
    kh_ref, vh_ref, sl_ref, mixed_ref, *, heads, scale,
):
    rows, width = q_ref.shape
    early = kh_ref.shape[0]
    hd = width // heads
    device = lax.axis_index(ALL)
    first_row = device * rows
    e2 = jnp.where(lax.rem(device, 4) < 2, far_ref[...].astype(F32), two_ref[...].astype(F32))
    e1 = jnp.where(lax.rem(device, 2) == 1, one_ref[...].astype(F32), cross_ref[...].astype(F32))
    xn = jnp.concatenate([normalize(e)[0].astype(BF) for e in (e2, e1)], axis=0)
    kh_ref[...] = jax.nn.silu(dot(xn, w_ref[:, 2 * width:3 * width])).astype(BF)
    vh_ref[...] = jax.nn.silu(dot(xn, w_ref[:, 3 * width:])).astype(BF)
    ends = history_ends(lengths_ref, first_row - early, (8, early))[0:1]
    row = lax.broadcasted_iota(jnp.int32, (rows, early), 0)
    share = jnp.where(row + first_row < ends, 1.0 / EV_DEV, 0.0)
    for h in range(heads):
        c = slice(h * hd, (h + 1) * hd)
        act, slope = silu_and_slope(dot_nt(q_ref[:, c], kh_ref[:, c]) * scale)
        wts = (act * share).astype(BF)
        sl_ref[h] = (slope * share).astype(BF)
        mixed_ref[:, c] = self_ref[:, c] + dot(wts, vh_ref[:, c])


def output_kernel(
    mixed_ref, ev_ref, pos_ref, up_ref, wo_ref,
    mine_ref, give_ref, normed_ref, inv_ref, unit_ref, target_ref, gated_ref, *, plane_cols,
):
    width = ev_ref.shape[1]
    normed_o, inv_o = normalize(mixed_ref[...])
    gated = (normed_o * up_ref[...].astype(F32)).astype(BF)
    normed_ref[...] = normed_o
    gated_ref[...] = gated
    dp_i, seq_n = lax.axis_index("dp"), lax.axis_size("seq")
    core = lax.rem(dp_i, 2)
    group = (dp_i // 2) * seq_n + lax.axis_index("seq")
    half = plane_cols // 2
    per = width // plane_cols if half else 0
    if not half:
        mine_ref[...] = gated
        give_ref[...] = gated[:, :give_ref.shape[1]]
    for j in range(half):
        g = group ^ j
        base = (g // seq_n) * 2 * seq_n + lax.rem(g, seq_n)
        a0 = pl.multiple_of((base + core * seq_n) * per, per)
        a1 = pl.multiple_of((base + (1 - core) * seq_n) * per, per)
        mine_ref[:, j * per:(j + 1) * per] = gated_ref[:, pl.ds(a0, per)]
        give_ref[:, j * per:(j + 1) * per] = gated_ref[:, pl.ds(a1, per)]
    layer_out = dot(gated, wo_ref[...]) + ev_ref[...].astype(F32)
    inv_norm = lax.rsqrt(jnp.sum(layer_out * layer_out, axis=1, keepdims=True))
    unit = layer_out * inv_norm
    positive = pos_ref[...].astype(F32)
    target = positive * lax.rsqrt(jnp.sum(positive * positive, axis=1, keepdims=True))
    pos_logit = jnp.sum(unit * target, axis=1, keepdims=True) / sharpness_divisor
    unit_ref[...] = unit
    target_ref[...] = target
    inv_ref[...] = jnp.concatenate([inv_o, inv_norm, pos_logit], axis=1)


def loss_kernel(
    unit_ref, target_ref, inv_ref, neg0_ref, neg1_ref, give_ref, pay_ref, gout_ref, low_ref,
):
    rows, width = unit_ref.shape
    unit, target = unit_ref[...], target_ref[...]
    inv_norm, pos_logit = inv_ref[:, 1:2], inv_ref[:, 2:3]
    neg = jnp.concatenate([neg0_ref[:, :width], neg1_ref[:, :width]], axis=0)
    logs = jnp.concatenate([neg0_ref[:, width:], neg1_ref[:, width:]], axis=0)
    lane = lax.broadcasted_iota(jnp.int32, (rows, logs.shape[1]), 1)
    offset = dot_nt(jnp.where(lane == 0, 1.0, 0.0).astype(BF), logs)
    neg_logit = dot_nt(unit.astype(BF), neg) / sharpness_divisor - offset
    exp_terms = jnp.exp(neg_logit)
    pos_exp = jnp.exp(pos_logit)
    total = pos_exp + jnp.sum(exp_terms, axis=1, keepdims=True)
    weighted = dot(exp_terms.astype(BF), neg)
    grad_unit = (loss_multiplier / sharpness_divisor) * (
        weighted / total + (pos_exp / total - 1.0) * target
    )
    grad_out = (grad_unit - unit * jnp.sum(unit * grad_unit, axis=1, keepdims=True)) * inv_norm
    gout_ref[...] = grad_out
    low = grad_out.astype(BF)
    low_ref[...] = low
    sent = pay_ref.shape[1] - width
    if sent:
        pay_ref[:, :sent] = give_ref[...]
    pay_ref[:, sent:] = low


def back_kernel(low_ref, normed_ref, inv_ref, su_ref, up_ref, wo_ref, gpu_ref, gm_ref):
    normed_o = normed_ref[...]
    grad_gated = dot_nt(low_ref[...], wo_ref[...])
    gpu_ref[...] = (grad_gated * normed_o * su_ref[...].astype(F32)).astype(BF)
    gm_ref[...] = norm_back(
        grad_gated * up_ref[...].astype(F32), normed_o, inv_ref[:, 0:1]
    ).astype(BF)


def product_kernel(mine_ref, pay_ref, got_ref, own_ref, *send_refs):
    cols = mine_ref.shape[1]
    per = cols // (len(send_refs) + 1)
    low = jnp.concatenate([pay_ref[:, cols:], got_ref[:, cols:]], axis=0)
    gated = jnp.concatenate([mine_ref[...], got_ref[:, :cols]], axis=0)
    out = dot_tn(gated, low)
    own_ref[...] = out[:per]
    for j, send_ref in enumerate(send_refs, 1):
        send_ref[...] = out[j * per:(j + 1) * per].astype(BF)


def sum_kernel(own_ref, *refs):
    *got_refs, kept_ref, give_ref = refs
    mid = kept_ref.shape[0]
    odd = lax.rem(lax.axis_index("pool"), 2) == 1
    total = own_ref[...]
    for got_ref in got_refs:
        total = total + got_ref[...].astype(F32)
    lower, upper = total[:mid], total[mid:]
    kept_ref[...] = jnp.where(odd, upper, lower)
    give_ref[...] = jnp.where(odd, lower, upper).astype(BF)


def join_kernel(kept_ref, got_ref, out_ref):
    mid = kept_ref.shape[0]
    odd = lax.rem(lax.axis_index("pool"), 2) == 1
    kept, got = kept_ref[...].astype(F32), got_ref[...].astype(F32)
    out_ref[:mid] = jnp.where(odd, got, kept)
    out_ref[mid:] = jnp.where(odd, kept, got)


def later_kernel(
    lengths_ref, one_ref, cross_ref, two_ref, far_ref, k_ref, w_ref,
    qn_ref, wn_ref, sn_ref, *, heads, scale,
):
    rows, width = k_ref.shape
    later = wn_ref.shape[0]
    hd = width // heads
    device = lax.axis_index(ALL)
    first_row = device * rows
    l1 = jnp.where(lax.rem(device, 2) == 1, cross_ref[...].astype(F32), one_ref[...].astype(F32))
    l2 = jnp.where(lax.rem(device, 4) < 2, two_ref[...].astype(F32), far_ref[...].astype(F32))
    xn = jnp.concatenate([normalize(e)[0].astype(BF) for e in (l1, l2)], axis=0)
    qn_ref[...] = jax.nn.silu(dot(xn, w_ref[:, width:2 * width])).astype(BF)
    ends = history_ends(lengths_ref, first_row, (8, rows))[0:1]
    row = lax.broadcasted_iota(jnp.int32, (later, rows), 0)
    share = jnp.where(row + (first_row + rows) < ends, 1.0 / EV_DEV, 0.0)
    for h in range(heads):
        c = slice(h * hd, (h + 1) * hd)
        act, slope = silu_and_slope(dot_nt(qn_ref[:, c], k_ref[:, c]) * scale)
        wn_ref[:, c] = (act * share).astype(BF)
        sn_ref[:, c] = (slope * share).astype(BF)


def middle_kernel(
    q_ref, k_ref, v_ref, kh_ref, vh_ref, ws_ref, ss_ref, sl_ref, gm_ref, sq_ref, gpu_ref, w_ref,
    dk_ref, dv_ref, gx_ref, *, heads, scale,
):
    width = q_ref.shape[1]
    hd = width // heads
    grad_q = []
    for h in range(heads):
        c = slice(h * hd, (h + 1) * hd)
        gm = gm_ref[:, c]
        ds = (dot_nt(gm, vh_ref[:, c]) * sl_ref[h].astype(F32)).astype(BF)
        ds_own = (dot_nt(gm, v_ref[:, c]) * ss_ref[h].astype(F32)).astype(BF)
        grad = dot(ds, kh_ref[:, c]) + dot(ds_own, k_ref[:, c])
        grad_q.append((grad * scale * sq_ref[:, c].astype(F32)).astype(BF))
        dk_ref[:, c] = dot_tn(ds_own, q_ref[:, c])
        dv_ref[:, c] = dot_tn(ws_ref[h], gm)
    gpq = jnp.concatenate(grad_q, axis=1)
    gx_ref[...] = dot_nt(gpu_ref[...], w_ref[:, :width]) + dot_nt(gpq, w_ref[:, width:2 * width])


def last_kernel(
    ev_ref, g1_ref, g1_odd_ref, g2_ref, g2_far_ref, qn_ref, wn_ref, sn_ref, k_ref, v_ref, dk_ref, dv_ref,
    sk_ref, sv_ref, w_ref, gx_ref, gout_ref, out_ref, *, heads, scale,
):
    width = ev_ref.shape[1]
    hd = width // heads
    grad_k, grad_v = [], []
    device = lax.axis_index(ALL)
    odd, within = lax.rem(device, 2) == 1, lax.rem(device, 4) < 2
    for h in range(heads):
        c = slice(h * hd, (h + 1) * hd)
        g2 = jnp.where(within, g2_ref[:, c].astype(F32), g2_far_ref[:, c].astype(F32))
        g1 = jnp.where(odd, g1_odd_ref[:, c].astype(F32), g1_ref[:, c].astype(F32))
        gm = jnp.concatenate([g1, g2], axis=0).astype(BF)
        ds = (dot_nt(gm, v_ref[:, c]) * sn_ref[:, c].astype(F32)).astype(BF)
        gk = (dk_ref[:, c] + dot_tn(ds, qn_ref[:, c])) * scale
        gv = dv_ref[:, c] + dot_tn(wn_ref[:, c], gm)
        grad_k.append((gk * sk_ref[:, c].astype(F32)).astype(BF))
        grad_v.append((gv * sv_ref[:, c].astype(F32)).astype(BF))
    grad_x = (
        gx_ref[...]
        + dot_nt(jnp.concatenate(grad_k, axis=1), w_ref[:, 2 * width:3 * width])
        + dot_nt(jnp.concatenate(grad_v, axis=1), w_ref[:, 3 * width:])
    )
    normed_x, inv_x = normalize(ev_ref[...].astype(F32))
    out_ref[...] = norm_back(grad_x, normed_x, inv_x) + gout_ref[...]


def call(kernel, outs, flops, *args, scalars=False, scratch=(), far=()):
    vmem = pl.BlockSpec(memory_space=pltpu.VMEM)
    specs = [vmem] * len(args)
    if scalars:
        specs[0] = pl.BlockSpec(memory_space=pltpu.SMEM)
    for i in far:
        specs[i] = pl.BlockSpec(memory_space=pltpu.HBM)
    return pl.pallas_call(
        kernel,
        in_specs=specs,
        out_specs=[vmem] * len(outs),
        out_shape=list(outs),
        scratch_shapes=list(scratch),
        cost_estimate=cost(flops, *args, *outs),
        compiler_params=pltpu.CompilerParams(vmem_limit_bytes=VMEM_BYTES),
    )(*args)


def shaped(shape, dtype):
    return jax.ShapeDtypeStruct(shape, dtype)


def cost(flops, *arrays):
    return pl.CostEstimate(
        flops=flops,
        bytes_accessed=sum(math.prod(x.shape) * x.dtype.itemsize for x in arrays),
        transcendentals=0,
    )


def layer(events, input_weight, output_weight, positives, negatives, log_probs, lengths):
    rows, width = events.shape
    hd = width // HEADS
    scale = 1.0 / math.sqrt(hd)
    early = REACH * rows
    low_block = shaped((rows, width), BF)
    wide_block = shaped((rows, width), F32)

    dp_n, seq_n = lax.axis_size("dp"), lax.axis_size("seq")
    plane_n = dp_n * seq_n
    half = plane_n // 2
    paired = width % (plane_n * 128) == 0 and is_pow2(half) and half > 0
    sent = width // 2 if paired else 0

    near = neighbours(events)
    part = negatives.shape[0] // plane_n
    if part % 16 == 0:
        piece, = call(
            piece_kernel, [shaped((part, width + 128), BF)], 0,
            negatives, log_probs[None, :],
        )
    else:
        at = lax.axis_index(PLANE) * part
        raw = lax.dynamic_slice_in_dim(negatives, at, part, 0).astype(F32)
        unit = raw * lax.rsqrt(jnp.sum(raw * raw, axis=1, keepdims=True))
        logs = lax.dynamic_slice_in_dim(log_probs, at, part, 0)
        piece = jnp.concatenate(
            [unit.astype(BF), jnp.broadcast_to(logs[:, None], (part, 128))], axis=1
        )
    neg0, neg1 = gathered(piece)

    flops = 2 * rows * width * width
    rows_x, up, q, k, v, s_up, s_q, s_k, s_v = call(
        own_kernel, [low_block] * 9, 4 * flops, events, input_weight
    )
    weight = input_weight

    early_block = shaped((early, width), BF)
    self_block, head_block = shaped((HEADS, rows, rows), BF), shaped((HEADS, rows, early), BF)
    self_weights, self_slopes, self_mixed = call(
        functools.partial(self_kernel, heads=HEADS, scale=scale),
        [self_block, self_block, wide_block], flops, lengths, q, k, v, scalars=True,
    )
    kh, vh, slopes, mixed = call(
        functools.partial(attend_kernel, heads=HEADS, scale=scale),
        [early_block, early_block, head_block, wide_block], 5 * flops,
        lengths, *near, q, self_mixed, weight, scalars=True,
    )
    mine, give, normed_o, inverses, unit, target = call(
        functools.partial(output_kernel, plane_cols=plane_n if paired else 0),
        [
            shaped((rows, sent or width), BF), shaped((rows, sent or 128), BF),
            wide_block, shaped((rows, 3), F32), wide_block, wide_block,
        ],
        flops, mixed, rows_x, positives, up, output_weight,
        scratch=[pltpu.VMEM((rows, width), BF)],
    )
    pay, grad_out, low = call(
        loss_kernel,
        [shaped((rows, sent + width), BF), wide_block, low_block],
        2 * flops, unit, target, inverses, neg0, neg1, give,
    )
    gpu, gm = call(
        back_kernel, [low_block, low_block],
        flops, low, normed_o, inverses, s_up, up, output_weight,
    )

    if paired:
        got = swapped(pay, "dp", 1)
        own_sum, *sends = call(
            product_kernel,
            [shaped((width // plane_n, width), F32)]
            + [shaped((width // plane_n, width), BF)] * (half - 1),
            flops, mine, pay, got,
        )
        terms = [own_sum]
        for j in range(1, half):
            pairs = []
            for i in range(plane_n):
                d, s = divmod(i, seq_n)
                t = ((d // 2) * seq_n + s) ^ j
                pairs.append((i, ((t // seq_n) * 2 + d % 2) * seq_n + t % seq_n))
            terms.append(lax.ppermute(sends[j - 1], PLANE, pairs))
    else:
        terms = [lax.psum_scatter(dot_tn(mine, pay), PLANE, scatter_dimension=0, tiled=True)]

    later = later_blocks(gm)

    qn, wn, sn = call(
        functools.partial(later_kernel, heads=HEADS, scale=scale),
        [early_block] * 3, 3 * flops, lengths, *near, k, weight, scalars=True,
    )
    dk, dv, gx = call(
        functools.partial(middle_kernel, heads=HEADS, scale=scale),
        [wide_block] * 3, 4 * flops,
        q, k, v, kh, vh, self_weights, self_slopes, slopes, gm, s_q, gpu, weight,
    )

    pool_n = lax.axis_size("pool")
    if is_pow2(pool_n) and pool_n > 2:
        rows_out = terms[0].shape[0]
        kept, give = call(
            sum_kernel,
            [shaped((rows_out // 2, width), F32), shaped((rows_out // 2, width), BF)], 0, *terms,
        )
        kept = kept + swapped(give, "pool", 1).astype(F32)
        for b in range(1, pool_n.bit_length() - 1):
            low = kept.astype(BF)
            kept = low.astype(F32) + swapped(low, "pool", 1 << b).astype(F32)
        low = kept.astype(BF)
        other = swapped(low, "pool", 1)
        total, = call(join_kernel, [shaped((rows_out, width), F32)], 0, low, other)
    else:
        total = lax.psum(sum(t.astype(F32) for t in terms), "pool")

    d_events, = call(
        functools.partial(last_kernel, heads=HEADS, scale=scale),
        [wide_block], 4 * flops,
        rows_x, *later, qn, wn, sn, k, v, dk, dv, s_k, s_v, weight, gx, grad_out,
    )
    return (d_events, total)


def solution(mesh):
    placed = (
        P(("dp", "seq", "pool"), None),
        P(),
        P(),
        P(("dp", "seq", "pool"), None),
        P("pool", None),
        P("pool"),
        P(),
    )
    return jax.shard_map(
        layer,
        mesh=mesh,
        in_specs=placed,
        out_specs=(P(("dp", "seq", "pool"), None), P(("dp", "seq"), None)),
        check_vma=False,
    )
```
